256 devices in a mesh: dp: 8 (over y, z_lo), shard: 32 (over x, z_hi, core).
Axes of the slice: x: 4, y: 4, z: 8 (z_hi: 4, z_lo: 2; z = z_hi * 2 + z_lo), core: 2. Of those that a mesh axis runs over, the one named last changes fastest.
Arguments:
- gradients: bfloat16 [8, 32, 8, 196608], P('dp', 'shard'), may hold values from -6 to 6
- tile_table: int32 [32, 96], replicated, may hold values from 0 to 3071, as said below
- master: float32 [32, 8, 196608], P('shard', 'dp'), may hold values from -0.072 to 0.072
- moment: float32 [32, 8, 196608], P('shard', 'dp'), may hold values from -6 to 6
- second: float32 [32, 8, 196608], P('shard', 'dp'), may hold values from 1 to 16
Outputs:
- master_new: float32 [32, 8, 196608], P('shard', 'dp')
- moment_new: float32 [32, 8, 196608], P('shard', 'dp')
- second_new: float32 [32, 8, 196608], P('shard', 'dp')
- tiles_out: bfloat16 [3072, 128, 128], P('shard')
- scales_out: bfloat16 [3072], P('shard')
The draws below stay inside these ranges and needn't reach their ends.
Inputs may be any that keep to these rules, and one draw needn't show every extreme that they name: tile_table holds each number of 0 to 3071 once; each row holds exactly 3 numbers of every block of 96 consecutive numbers; in any row, the columns d * 12 to (d + 1) * 12 - 1 hold at most 1 numbers of one block, and this most is reached; over all rows together those columns hold exactly 12 numbers of every block.
All inputs are finite; a program needn't handle non-finite values.
Results may differ from the reference program's by a relative error of at most 0.0095.
Values may be sent and summed in bfloat16 or wider, within the bound.
A program may use at most 64 MiB of HBM per device.

```python
import math
import jax
import jax.numpy as jnp
from jax import lax

TB = 128
TILES_OWNER = 96
SHARD_LEN = 196608
N_DP = 8
N_SHARD = 32


def shuffle_row(key, row_values):
    return jax.random.permutation(key, row_values)


def owner_permutation(key):
    return jax.random.permutation(key, TILES_OWNER)


def draw_tile_table(key, part):
    sub_len = TILES_OWNER // N_DP
    per_pair = TILES_OWNER // N_SHARD
    shifts = jax.random.permutation(jax.random.fold_in(key, 31), N_SHARD).astype(jnp.int32)
    relabel = jax.random.permutation(jax.random.fold_in(key, 32), N_SHARD).astype(jnp.int32)
    position = jnp.arange(TILES_OWNER, dtype=jnp.int32)
    cyclic = (position[None, :] + shifts[:, None]) % N_SHARD
    labels = relabel[cyclic].reshape(N_SHARD * N_DP, sub_len)
    block_keys = jax.random.split(jax.random.fold_in(key, 33), N_SHARD * N_DP)
    labels = jax.vmap(shuffle_row)(block_keys, labels).reshape(N_SHARD, TILES_OWNER).astype(jnp.int32)
    same = labels[:, :, None] == labels[:, None, :]
    earlier = position[None, :] < position[:, None]
    row_rank = jnp.sum(jnp.logical_and(same, earlier[None]), axis=-1).astype(jnp.int32)
    occurrence = jnp.arange(N_SHARD, dtype=jnp.int32)[:, None] * per_pair + row_rank
    owner_keys = jax.random.split(jax.random.fold_in(key, 34), N_SHARD)
    perms = jax.vmap(owner_permutation)(owner_keys).astype(jnp.int32)
    slots = labels * TILES_OWNER + perms[labels, occurrence]
    return slots.astype(jnp.int32)


def draw_master(key, part):
    shape = (N_SHARD, N_DP, SHARD_LEN // TB, TB)
    base = jnp.clip(jax.random.normal(jax.random.fold_in(key, 21), shape, jnp.float32), -6.0, 6.0)
    row_scale = jnp.exp(jax.random.uniform(jax.random.fold_in(key, 22), shape[:3] + (1,), jnp.float32, 0.0, math.log(10.0)))
    factor = 0.0012
    values = factor * base * row_scale
    return values.reshape(N_SHARD, N_DP, SHARD_LEN).astype(jnp.float32)


def spiked(values, rng, source, target, shards_of, factor):
    owner, partner = [(jnp.arange(values.shape[dim]) // (values.shape[dim] // shards_of)).reshape([-1 if axis == dim else 1 for axis in range(values.ndim)]) for dim in (source, target)]
    chosen = jax.random.permutation(rng, shards_of)[partner]
    strong = (owner == chosen) | (owner == (partner + shards_of // 2) % shards_of)
    return jnp.where(strong, factor * values, values)


def block_levels(own_key, dims, shards, low, high):
    level = 1.0
    for dim, shards_of in shards:
        heights = jax.random.uniform(jax.random.fold_in(jax.random.fold_in(own_key, 6), dim), (shards_of,), jnp.float32, low / len(shards), high / len(shards))
        level = level * jnp.repeat(jnp.exp(heights), dims[dim] // shards_of).reshape((-1,) + (1,) * (len(dims) - 1 - dim))
    return level


def noise(rng, shape, spread, most, pieces=(), kind=jnp.bfloat16):
    drawn = spread * jax.random.normal(rng, shape, jnp.float32)
    if pieces:
        drawn = drawn * block_levels(rng, shape, pieces, -0.22, 0.18)
    return jnp.clip(drawn, -most, most).astype(kind)


def heavy_noise(own_key, shape, deviation, reach, shards, heavy, kind=jnp.bfloat16):
    result = deviation * jax.random.normal(own_key, shape, jnp.float32)
    if shards:
        result = result * block_levels(own_key, shape, shards, -0.22, 0.18)
    return jnp.clip(spiked(result, jax.random.fold_in(own_key, 3), *heavy), -reach, reach).astype(kind)


def setup_inputs(seed: int = 0) -> dict:
    key_list = jax.random.split(jax.random.key(seed), 6)
    return {
        "gradients": heavy_noise(key_list[0], (N_DP, N_SHARD, N_DP, SHARD_LEN), 1.0, 6.0, ((0, 8), (1, 32)), (0, 2, 8, 2.0)),
        "tile_table": draw_tile_table(jax.random.fold_in(key_list[5], 71), 0),
        "master": draw_master(jax.random.fold_in(key_list[5], 71), 0),
        "moment": noise(key_list[3], (N_SHARD, N_DP, SHARD_LEN), 1.0, 6.0, ((0, 32), (1, 8)), jnp.float32),
        "second": jnp.clip(jnp.exp(math.log(16.0) - 2.7725887 * jax.random.uniform(key_list[4], (N_SHARD, N_DP, SHARD_LEN), jnp.float32) ** block_levels(key_list[4], (N_SHARD, N_DP, SHARD_LEN), ((0, 32), (1, 8)), -0.2, 0.2)), 1.0, 16.0),
    }


beta_first = 0.9
beta_second = 0.95
learning_rate = 0.002
weight_decay = 0.1
adam_epsilon = 1e-08
scale_epsilon = 1e-06
step_count = 10

def reference(gradients, tile_table, master, moment, second):
    grad = lax.optimization_barrier(jnp.sum(gradients.astype(jnp.float32), axis=0))
    moment_new = beta_first * moment + (1.0 - beta_first) * grad
    second_new = beta_second * second + (1.0 - beta_second) * grad * grad
    first_fix = 1.0 - beta_first ** step_count
    second_fix = 1.0 - beta_second ** step_count
    update = moment_new / first_fix / (jnp.sqrt(second_new / second_fix) + adam_epsilon)
    master_new = master - learning_rate * (update + weight_decay * master)
    tile_set = master_new.reshape(-1, TB, TB)
    largest = lax.optimization_barrier(jnp.max(jnp.abs(tile_set), axis=(1, 2)))
    tile_scale = (largest + scale_epsilon).astype(jnp.bfloat16)
    quantized = (tile_set / tile_scale.astype(jnp.float32)[:, None, None]).astype(jnp.bfloat16)
    slots = tile_table.reshape(-1).astype(jnp.int32)
    tiles_out = jnp.zeros_like(quantized).at[slots].set(quantized)
    scales_out = jnp.zeros(tile_scale.shape, jnp.bfloat16).at[slots].set(tile_scale)
    return (master_new, moment_new, second_new, tiles_out, scales_out)
```

```python
import functools

import jax
import jax.numpy as jnp
from jax import lax
from jax.experimental import pallas as pl
from jax.experimental.pallas import tpu as pltpu
from jax.sharding import PartitionSpec as P

TB = 128
beta_first = 0.9
beta_second = 0.95
learning_rate = 0.002
weight_decay = 0.1
adam_epsilon = 1e-08
scale_epsilon = 1e-06
step_count = 10

MESH = pl.DeviceIdType.MESH
N_DP = 8
N_SH = 32
NT = 12
OWNED = 96
PIECES = 4
PR = TB // PIECES


def wait_bytes(ref, sem):
    pltpu.make_async_copy(ref, ref, sem).wait()


def lane_sum(x):
    return jnp.sum(x, axis=1, keepdims=True)


def index_tables(tab_ref, idx_ref, place_ref, me_sh, me_dp):
    def iota(shape, dim):
        return lax.broadcasted_iota(jnp.int32, shape, dim)

    lane32 = iota((N_SH, OWNED), 1)
    row32 = iota((N_SH, OWNED), 0)
    mine = tab_ref[pl.ds(me_sh, 1), :]
    owner = ((mine >> 5) * 171) >> 9
    offset = jnp.broadcast_to((owner - me_sh - 1) & (N_SH - 1), (N_SH, OWNED))
    col = lane32 - me_dp * NT
    hit = (offset == row32) & (col >= 0) & (col < NT)
    idx_ref[0:N_SH, :] = jnp.broadcast_to(jnp.minimum(lane_sum(jnp.where(hit, col, 0)), NT - 1), (N_SH, TB))

    slot = iota((OWNED, OWNED), 0)
    lane = iota((OWNED, OWNED), 1)
    wanted = slot + me_sh * OWNED

    def find(j, acc):
        row = jnp.broadcast_to(tab_ref[pl.ds(j, 1), :], (OWNED, OWNED))
        return acc + jnp.where(row == wanted, lane + j * TB, 0)

    found = lane_sum(lax.fori_loop(0, N_SH, find, jnp.zeros((OWNED, OWNED), jnp.int32)))
    found = jnp.broadcast_to(found, (OWNED, OWNED))
    source = found >> 7
    part = ((found & (TB - 1)) * 43) >> 9

    def as_row(x):
        return jnp.sum(jnp.where(slot == lane, x, 0), axis=0, keepdims=True)

    part_row = jnp.broadcast_to(as_row(part), (OWNED, OWNED))
    rank = lane_sum(jnp.where((part_row == part) & (lane < slot), 1, 0))
    rank = jnp.broadcast_to(rank, (OWNED, OWNED))
    place_ref[...] = jnp.broadcast_to(jnp.clip(part * NT + rank, 0, OWNED - 1)[:, 0:1], (OWNED, TB))
    arrival = as_row((me_sh - source - 1) & (N_SH - 1))
    key = as_row(jnp.where(part == me_dp, rank, -1))
    row16 = iota((16, OWNED), 0)
    pick = jnp.where(jnp.broadcast_to(key, (16, OWNED)) == row16, jnp.broadcast_to(arrival, (16, OWNED)), 0)
    idx_ref[N_SH : N_SH + 16, :] = jnp.broadcast_to(lane_sum(pick) & (N_SH - 1), (16, TB))


def adam(grad, master, moment, second):
    moment_new = beta_first * moment + (1.0 - beta_first) * grad
    second_new = beta_second * second + (1.0 - beta_second) * grad * grad
    first_fix = 1.0 - beta_first**step_count
    second_fix = 1.0 - beta_second**step_count
    update = moment_new / first_fix / (jnp.sqrt(second_new / second_fix) + adam_epsilon)
    master_new = master - learning_rate * (update + weight_decay * master)
    return master_new, moment_new, second_new


def main_kernel(
    g_hbm, tab_ref, master_hbm, moment_hbm, second_hbm,
    master_out, moment_out, second_out, whole, whole_s, place,
    g_v, spread, snd, rcv, master_v, moment_v, second_v, quant, scale, stage, stage_s, arrive_s, idx_v, idx_s, *rest,
):
    arrive = rest[:PIECES]
    in_sem, st_sem, idx_sem, rs_send, rs_recv, sh_send, sh_recv, ss_send, ss_recv, ag_send, ag_recv, as_send, as_recv = rest[PIECES:]
    me_dp = lax.axis_index("dp")
    me_sh = lax.axis_index("shard")

    def dp_peer(k):
        return lax.rem(me_dp + k, N_DP)

    def sh_peer(k):
        return lax.rem(me_sh + k, N_SH)

    cols = TB * TB

    def load_gradient(t):
        at = pl.ds(pl.multiple_of(t * cols, cols), cols)
        return pltpu.make_async_copy(g_hbm.at[:, at], g_v.at[:, at], in_sem.at[t])

    for t in range(NT):
        load_gradient(t).start()
    states = [
        pltpu.make_async_copy(a, b, st_sem.at[i])
        for i, (a, b) in enumerate(((master_hbm, master_v), (moment_hbm, moment_v), (second_hbm, second_v)))
    ]
    for copy in states:
        copy.start()

    barrier = pltpu.get_barrier_semaphore()
    for k in range(1, N_DP):
        pl.semaphore_signal(barrier, 1, device_id={"dp": dp_peer(k)}, device_id_type=MESH)
    for k in range(1, N_SH):
        pl.semaphore_signal(barrier, 1, device_id={"shard": sh_peer(k)}, device_id_type=MESH)

    def split_rows(t):
        load_gradient(t).wait()

        def group(c, _):
            at = pl.multiple_of(t * cols + c * 2048, 2048)
            for u in range(16):
                spread[u * 8 : u * 8 + 8, :] = g_v[:, pl.ds(at + u * TB, TB)].astype(jnp.float32)
            for i in range(N_DP):
                snd[i, t, pl.ds(pl.multiple_of(c * 16, 16), 16), :] = spread[pl.ds(i, 16, stride=8), :].astype(jnp.bfloat16)
            return 0

        lax.fori_loop(0, 8, group, 0)

    def scatter_copy(t, k):
        return pltpu.make_async_remote_copy(
            snd.at[dp_peer(k), t], rcv.at[k, t], rs_send.at[t], rs_recv.at[t],
            device_id={"dp": dp_peer(k)}, device_id_type=MESH,
        )

    def scatter(t):
        for k in range(1, N_DP):
            scatter_copy(t, k).start()

    split_rows(0)
    pl.semaphore_wait(barrier, N_DP - 1 + N_SH - 1)
    scatter(0)

    def scatter_step(t, _):
        split_rows(t)
        scatter(t)
        return 0

    lax.fori_loop(1, NT, scatter_step, 0)

    index_tables(tab_ref, idx_v, place, me_sh, me_dp)
    idx_copy = pltpu.make_async_copy(idx_v, idx_s, idx_sem)
    idx_copy.start()
    idx_copy.wait()
    for copy in states:
        copy.wait()

    def update_step(t, _):
        wait_bytes(rcv.at[pl.ds(1, N_DP - 1), t], rs_recv.at[t])

        def rows_step(b, largest):
            at = pl.ds(pl.multiple_of(b * 32, 32), 32)
            flat = pl.ds(pl.multiple_of(t * TB + b * 32, 32), 32)
            grad = snd[me_dp, t, at, :].astype(jnp.float32)
            for k in range(1, N_DP):
                grad = grad + rcv[k, t, at, :].astype(jnp.float32)
            new = adam(grad, master_v[flat, :], moment_v[flat, :], second_v[flat, :])
            master_out[flat, :], moment_out[flat, :], second_out[flat, :] = new
            return jnp.maximum(largest, jnp.abs(new[0]))

        largest = lax.fori_loop(0, TB // 32, rows_step, jnp.zeros((32, TB), jnp.float32))
        largest = jnp.max(jnp.max(largest, axis=0, keepdims=True), axis=1, keepdims=True)
        tile_scale = (jnp.broadcast_to(largest, (16, TB)) + scale_epsilon).astype(jnp.bfloat16).astype(jnp.float32)
        scale[t] = tile_scale[0:1, :]
        divisor = jnp.broadcast_to(tile_scale[0:1, :], (TB, TB))
        quant[t] = (master_out[pl.ds(pl.multiple_of(t * TB, TB), TB), :] / divisor).astype(jnp.bfloat16)
        return 0

    lax.fori_loop(0, NT, update_step, 0)

    def shard_copy(p, k):
        return pltpu.make_async_remote_copy(
            stage.at[p, k - 1], arrive[p].at[k - 1], sh_send.at[p], sh_recv.at[p],
            device_id={"shard": sh_peer(k)}, device_id_type=MESH,
        )

    def scale_copy(k):
        return pltpu.make_async_remote_copy(
            stage_s.at[k - 1], arrive_s.at[k - 1], ss_send, ss_recv,
            device_id={"shard": sh_peer(k)}, device_id_type=MESH,
        )

    for p in range(PIECES):
        rows = slice(p * PR, (p + 1) * PR)

        def stage_step(k, _, p=p, rows=rows):
            stage[p, k - 1] = quant[idx_s[k - 1, 0], rows, :]
            if p == 0:
                stage_s[k - 1] = scale[idx_s[k - 1, 0]]
                scale_copy(k).start()
            shard_copy(p, k).start()
            return 0

        lax.fori_loop(1, N_SH, stage_step, 0)
        arrive[p][N_SH - 1] = quant[idx_s[N_SH - 1, 0], rows, :]
    arrive_s[N_SH - 1] = scale[idx_s[N_SH - 1, 0]]

    def gather_copy(p, k):
        return pltpu.make_async_remote_copy(
            whole.at[p, me_dp], whole.at[p, me_dp], ag_send.at[p, k], ag_recv.at[p, k],
            device_id={"dp": dp_peer(k)}, device_id_type=MESH,
        )

    def gather_scale_copy(k):
        return pltpu.make_async_remote_copy(
            whole_s.at[me_dp], whole_s.at[me_dp], as_send.at[k], as_recv.at[k],
            device_id={"dp": dp_peer(k)}, device_id_type=MESH,
        )

    wait_bytes(arrive_s.at[pl.ds(0, N_SH - 1)], ss_recv)
    for i in range(NT):
        whole_s[me_dp, i] = arrive_s[idx_s[N_SH + i, 0]]
    for k in range(1, N_DP):
        gather_scale_copy(k).start()
    for p in range(PIECES):
        wait_bytes(arrive[p].at[pl.ds(0, N_SH - 1)], sh_recv.at[p])
        for i in range(NT):
            whole[p, me_dp, i] = arrive[p][idx_s[N_SH + i, 0]]
        for k in range(1, N_DP):
            gather_copy(p, k).start()

    def finish(t, _):
        for k in range(1, N_DP):
            scatter_copy(t, k).wait_send()
        return 0

    lax.fori_loop(0, NT, finish, 0)
    wait_bytes(stage_s.at[pl.ds(0, N_SH - 1)], ss_send)
    for p in range(PIECES):
        wait_bytes(stage.at[p, pl.ds(0, N_SH - 1)], sh_send.at[p])
    for k in range(1, N_DP):
        gather_scale_copy(k).wait()
        for p in range(PIECES):
            gather_copy(p, k).wait()


def place_kernel(whole, whole_s, place, master_v, moment_v, second_v, tiles, scales, master_out, moment_out, second_out, sem, tile_sem):
    copies = [
        pltpu.make_async_copy(a, b, sem.at[i])
        for i, (a, b) in enumerate(((master_v, master_out), (moment_v, moment_out), (second_v, second_out)))
    ]

    def start(s, _):
        pltpu.make_async_copy(whole.at[:, place[s, 0]], tiles.at[s], tile_sem).start()
        return 0

    lax.fori_loop(0, OWNED, start, 0)
    for copy in copies:
        copy.start()
    lane = lax.broadcasted_iota(jnp.int32, (1, TB), 1)

    def collect(s, acc):
        return jnp.where(lane == s, whole_s[place[s, 0]], acc)

    row = lax.fori_loop(0, OWNED, collect, jnp.zeros((1, TB), jnp.float32))
    scales[...] = row.astype(jnp.bfloat16)
    wait_bytes(tiles, tile_sem)
    for copy in copies:
        copy.wait()


def per_device(gradients, tile_table, master, moment, second):
    shape = master.shape
    flat = (NT * TB, TB)
    f32, bf16 = jnp.float32, jnp.bfloat16
    anywhere = pl.BlockSpec(memory_space=pltpu.HBM)
    vmem = pl.BlockSpec(memory_space=pltpu.VMEM)
    smem = pl.BlockSpec(memory_space=pltpu.SMEM)
    dma = pltpu.SemaphoreType.DMA
    state = jax.ShapeDtypeStruct(flat, f32)
    tile = (TB, TB)
    outs = pl.pallas_call(
        main_kernel,
        out_shape=(
            pltpu.VMEM(flat, f32), pltpu.VMEM(flat, f32), pltpu.VMEM(flat, f32),
            pltpu.VMEM((PIECES, N_DP, NT, PR, TB), bf16),
            pltpu.VMEM((N_DP, NT, 1, TB), f32),
            pltpu.VMEM((OWNED, TB), jnp.int32),
        ),
        in_specs=[anywhere, vmem, anywhere, anywhere, anywhere],
        out_specs=(vmem,) * 6,
        scratch_shapes=[
            pltpu.VMEM((N_DP, NT * TB * TB), bf16),
            pltpu.VMEM((TB, TB), f32),
            pltpu.VMEM((N_DP, NT) + tile, bf16),
            pltpu.VMEM((N_DP, NT) + tile, bf16),
            pltpu.VMEM(flat, f32), pltpu.VMEM(flat, f32), pltpu.VMEM(flat, f32),
            pltpu.VMEM((NT,) + tile, bf16),
            pltpu.VMEM((NT, 1, TB), f32),
            pltpu.VMEM((PIECES, N_SH, PR, TB), bf16),
            pltpu.VMEM((N_SH, 1, TB), f32),
            pltpu.VMEM((N_SH, 1, TB), f32),
            pltpu.VMEM((48, TB), jnp.int32),
            pltpu.SMEM((48, TB), jnp.int32),
            *[pltpu.VMEM((N_SH, PR, TB), bf16) for _ in range(PIECES)],
            dma((NT,)), dma((3,)), dma(()),
            dma((NT,)), dma((NT,)),
            dma((PIECES,)), dma((PIECES,)),
            dma(()), dma(()),
            dma((PIECES, N_DP)), dma((PIECES, N_DP)),
            dma((N_DP,)), dma((N_DP,)),
        ],
        compiler_params=pltpu.CompilerParams(collective_id=0, has_side_effects=True, vmem_limit_bytes=58 << 20),
    )(
        gradients.reshape(N_DP, NT * TB * TB), tile_table,
        master.reshape(flat), moment.reshape(flat), second.reshape(flat),
    )
    master_new, moment_new, second_new, whole, whole_s, place = outs
    tiles, scales, master_new, moment_new, second_new = pl.pallas_call(
        place_kernel,
        out_shape=(
            jax.ShapeDtypeStruct((OWNED, PIECES, PR, TB), bf16),
            jax.ShapeDtypeStruct((1, TB), bf16),
            state, state, state,
        ),
        in_specs=[vmem, vmem, smem, vmem, vmem, vmem],
        out_specs=(anywhere, vmem, anywhere, anywhere, anywhere),
        scratch_shapes=[dma((3,)), dma(())],
        compiler_params=pltpu.CompilerParams(vmem_limit_bytes=16 << 20),
    )(whole.reshape(PIECES, OWNED, PR, TB), whole_s.reshape(OWNED, 1, TB), place, master_new, moment_new, second_new)
    return (
        master_new.reshape(shape), moment_new.reshape(shape), second_new.reshape(shape),
        tiles.reshape(OWNED, TB, TB), scales[0, :OWNED],
    )


def solution(mesh):
    in_specs = (
        P("dp", "shard", None, None),
        P(),
        P("shard", "dp", None),
        P("shard", "dp", None),
        P("shard", "dp", None),
    )
    out_specs = (
        P("shard", "dp", None),
        P("shard", "dp", None),
        P("shard", "dp", None),
        P("shard", None, None),
        P("shard"),
    )
    return jax.shard_map(
        per_device, mesh=mesh, in_specs=in_specs, out_specs=out_specs, check_vma=False
    )
```

```python
import functools

import jax
import jax.numpy as jnp
from jax import lax
from jax.experimental import pallas as pl
from jax.experimental.pallas import tpu as pltpu
from jax.sharding import PartitionSpec as P

TB = 128
beta_first = 0.9
beta_second = 0.95
learning_rate = 0.002
weight_decay = 0.1
adam_epsilon = 1e-08
scale_epsilon = 1e-06
step_count = 10

MESH = pl.DeviceIdType.MESH
N_DP = 8
N_SH = 32
NT = 12
OWNED = 96
NZ = 7
NY = NT - NZ
PIECES = 4
AHEAD = 2
PR = TB // PIECES


def wait_bytes(ref, sem):
    pltpu.make_async_copy(ref, ref, sem).wait()


def lane_sum(x):
    return jnp.sum(x, axis=1, keepdims=True)


def index_tables(tab_ref, idx_ref, place_ref, me_sh, me_dp):
    def iota(shape, dim):
        return lax.broadcasted_iota(jnp.int32, shape, dim)

    lane32 = iota((N_SH, OWNED), 1)
    row32 = iota((N_SH, OWNED), 0)
    mine = tab_ref[pl.ds(me_sh, 1), :]
    owner = ((mine >> 5) * 171) >> 9
    offset = jnp.broadcast_to((owner - me_sh - 1) & (N_SH - 1), (N_SH, OWNED))
    col = lane32 - me_dp * NT
    hit = (offset == row32) & (col >= 0) & (col < NT)
    idx_ref[0:N_SH, :] = jnp.broadcast_to(jnp.minimum(lane_sum(jnp.where(hit, col, 0)), NT - 1), (N_SH, TB))

    slot = iota((OWNED, OWNED), 0)
    lane = iota((OWNED, OWNED), 1)
    wanted = slot + me_sh * OWNED

    def find(j, acc):
        row = jnp.broadcast_to(tab_ref[pl.ds(j, 1), :], (OWNED, OWNED))
        return acc + jnp.where(row == wanted, lane + j * TB, 0)

    found = lane_sum(lax.fori_loop(0, N_SH, find, jnp.zeros((OWNED, OWNED), jnp.int32)))
    found = jnp.broadcast_to(found, (OWNED, OWNED))
    source = found >> 7
    part = ((found & (TB - 1)) * 43) >> 9

    def as_row(x):
        return jnp.sum(jnp.where(slot == lane, x, 0), axis=0, keepdims=True)

    part_row = jnp.broadcast_to(as_row(part), (OWNED, OWNED))
    rank = lane_sum(jnp.where((part_row == part) & (lane < slot), 1, 0))
    rank = jnp.broadcast_to(rank, (OWNED, OWNED))
    place_ref[...] = jnp.broadcast_to(jnp.clip(part * NT + rank, 0, OWNED - 1)[:, 0:1], (OWNED, TB))
    arrival = as_row((me_sh - source - 1) & (N_SH - 1))
    key = as_row(jnp.where(part == me_dp, rank, -1))
    row16 = iota((16, OWNED), 0)
    pick = jnp.where(jnp.broadcast_to(key, (16, OWNED)) == row16, jnp.broadcast_to(arrival, (16, OWNED)), 0)
    idx_ref[N_SH : N_SH + 16, :] = jnp.broadcast_to(lane_sum(pick) & (N_SH - 1), (16, TB))


def adam(grad, master, moment, second):
    moment_new = beta_first * moment + (1.0 - beta_first) * grad
    second_new = beta_second * second + (1.0 - beta_second) * grad * grad
    first_fix = 1.0 - beta_first**step_count
    second_fix = 1.0 - beta_second**step_count
    update = moment_new / first_fix / (jnp.sqrt(second_new / second_fix) + adam_epsilon)
    master_new = master - learning_rate * (update + weight_decay * master)
    return master_new, moment_new, second_new


def main_kernel(
    g_hbm, tab_ref, master_hbm, moment_hbm, second_hbm,
    master_out, moment_out, second_out, whole, whole_s, place,
    g_v, spread, z_own, z_got, z_part, z_last, y_own, y_got, y_part, y_last,
    master_v, moment_v, second_v, quant, scale, stage, stage_s, arrive_s, idx_v, idx_s, *rest,
):
    arrive = rest[:PIECES]
    (
        in_sem, st_sem, idx_sem,
        z1_send, z1_recv, z2_send, z2_recv, y1_send, y1_recv, y2_send, y2_recv,
        sh_send, sh_recv, ss_send, ss_recv, ag_send, ag_recv, as_send, as_recv,
    ) = rest[PIECES:]
    me_dp = lax.axis_index("dp")
    me_sh = lax.axis_index("shard")
    me_y, me_z = me_dp // 2, me_dp % 2

    def dp_peer(k):
        return lax.rem(me_dp + k, N_DP)

    def sh_peer(k):
        return lax.rem(me_sh + k, N_SH)

    def y_peer(k):
        return lax.rem(me_y + k, 4)

    def to_dp(d):
        return dict(device_id={"dp": d}, device_id_type=MESH)

    z_mate = me_y * 2 + 1 - me_z
    cols = TB * TB
    f32, bf16 = jnp.float32, jnp.bfloat16

    order = []
    for i in range(max(NZ, NY)):
        order += [("y", i)] * (i < NY) + [("z", i)] * (i < NZ)

    def tile_of(item):
        return item[1] + (NZ if item[0] == "y" else 0)

    def load_gradient(t):
        at = pl.ds(t * cols, cols)
        return pltpu.make_async_copy(g_hbm.at[:, at], g_v.at[:, at], in_sem.at[t])

    for item in order:
        load_gradient(tile_of(item)).start()
    states = [
        pltpu.make_async_copy(a, b, st_sem.at[i])
        for i, (a, b) in enumerate(((master_hbm, master_v), (moment_hbm, moment_v), (second_hbm, second_v)))
    ]
    for copy in states:
        copy.start()

    barrier = pltpu.get_barrier_semaphore()
    for k in range(1, N_DP):
        pl.semaphore_signal(barrier, 1, device_id={"dp": dp_peer(k)}, device_id_type=MESH)
    for k in range(1, N_SH):
        pl.semaphore_signal(barrier, 1, device_id={"shard": sh_peer(k)}, device_id_type=MESH)

    def split_rows(item):
        t = tile_of(item)
        load_gradient(t).wait()

        def group(c, _):
            at = pl.multiple_of(t * cols + c * 2048, 2048)
            for u in range(16):
                spread[u * 8 : u * 8 + 8, :] = g_v[:, pl.ds(at + u * TB, TB)].astype(f32)
            rows = pl.ds(pl.multiple_of(c * 16, 16), 16)
            for i in range(N_DP):
                value = spread[pl.ds(i, 16, stride=8), :].astype(bf16)
                if item[0] == "z":
                    z_own[i % 2, item[1], i // 2, rows, :] = value
                else:
                    y_own[item[1], i // 2, i % 2, rows, :] = value
            return 0

        lax.fori_loop(0, 8, group, 0)

    def z1_copy(a):
        return pltpu.make_async_remote_copy(
            z_own.at[1 - me_z, a], z_got.at[a], z1_send.at[a], z1_recv.at[a], **to_dp(z_mate))

    def z2_copy(a, k):
        return pltpu.make_async_remote_copy(
            z_part.at[a, k - 1], z_last.at[a, k - 1], z2_send.at[a], z2_recv.at[a],
            **to_dp(y_peer(k) * 2 + me_z))

    def y1_copy(b, k):
        return pltpu.make_async_remote_copy(
            y_own.at[b, y_peer(k)], y_got.at[b, k - 1], y1_send.at[b], y1_recv.at[b],
            **to_dp(y_peer(k) * 2 + me_z))

    def y2_copy(b):
        return pltpu.make_async_remote_copy(
            y_part.at[b], y_last.at[b], y2_send.at[b], y2_recv.at[b], **to_dp(z_mate))

    def first_sends(item):
        if item[0] == "z":
            z1_copy(item[1]).start()
        else:
            for k in (1, 3, 2):
                y1_copy(item[1], k).start()

    split_rows(order[0])
    split_rows(order[1])
    pl.semaphore_wait(barrier, N_DP - 1 + N_SH - 1)
    first_sends(order[0])
    first_sends(order[1])
    for item in order[2:]:
        split_rows(item)
        first_sends(item)

    index_tables(tab_ref, idx_v, place, me_sh, me_dp)
    idx_copy = pltpu.make_async_copy(idx_v, idx_s, idx_sem)
    idx_copy.start()
    idx_copy.wait()
    for copy in states:
        copy.wait()

    def blocks(body, init=0):
        return lax.fori_loop(0, TB // 32, lambda b, c: body(pl.ds(pl.multiple_of(b * 32, 32), 32), b, c), init)

    def middle(item):
        i = item[1]
        if item[0] == "z":
            wait_bytes(z_got.at[i], z1_recv.at[i])

            def add(rows, b, _):
                for k in (1, 3, 2):
                    y = y_peer(k)
                    z_part[i, k - 1, rows, :] = (
                        z_own[me_z, i, y, rows, :].astype(f32) + z_got[i, y, rows, :].astype(f32)
                    ).astype(bf16)
                return 0

            blocks(add)
            for k in (1, 3, 2):
                z2_copy(i, k).start()
        else:
            wait_bytes(y_got.at[i], y1_recv.at[i])

            def add(rows, b, _):
                other = y_own[i, me_y, 1 - me_z, rows, :].astype(f32)
                for k in range(3):
                    other = other + y_got[i, k, 1 - me_z, rows, :].astype(f32)
                y_part[i, rows, :] = other.astype(bf16)
                return 0

            blocks(add)
            y2_copy(i).start()

    def last(item):
        i, t = item[1], tile_of(item)
        if item[0] == "z":
            wait_bytes(z_last.at[i], z2_recv.at[i])
        else:
            wait_bytes(y_last.at[i], y2_recv.at[i])

        def step(rows, b, largest):
            flat = pl.ds(pl.multiple_of(t * TB + b * 32, 32), 32)
            if item[0] == "z":
                terms = [z_own[me_z, i, me_y, rows, :], z_got[i, me_y, rows, :]]
                terms += [z_last[i, k, rows, :] for k in range(3)]
            else:
                terms = [y_own[i, me_y, me_z, rows, :]] + [y_got[i, k, me_z, rows, :] for k in range(3)]
                terms += [y_last[i, rows, :]]
            grad = functools.reduce(lambda a, b: a + b, [x.astype(f32) for x in terms])
            new = adam(grad, master_v[flat, :], moment_v[flat, :], second_v[flat, :])
            master_out[flat, :], moment_out[flat, :], second_out[flat, :] = new
            return jnp.maximum(largest, jnp.abs(new[0]))

        largest = blocks(step, jnp.zeros((32, TB), f32))
        largest = jnp.max(jnp.max(largest, axis=0, keepdims=True), axis=1, keepdims=True)
        tile_scale = (jnp.broadcast_to(largest, (16, TB)) + scale_epsilon).astype(bf16).astype(f32)
        scale[t] = tile_scale[0:1, :]
        divisor = jnp.broadcast_to(tile_scale[0:1, :], (TB, TB))
        quant[t] = (master_out[t * TB : (t + 1) * TB, :] / divisor).astype(bf16)

    for act, item in (
        [(middle, x) for x in order[:10]]
        + [(last, ("z", 0)), (middle, ("z", 5)), (last, ("z", 1)), (last, ("z", 2)), (middle, ("z", 6))]
        + [(last, x) for x in (("z", 3), ("z", 4), ("y", 0), ("y", 1), ("y", 2), ("z", 5), ("y", 3), ("y", 4), ("z", 6))]
    ):
        act(item)

    def shard_copy(p, k):
        return pltpu.make_async_remote_copy(
            stage.at[p, k - 1], arrive[p].at[k - 1], sh_send.at[p], sh_recv.at[p],
            device_id={"shard": sh_peer(k)}, device_id_type=MESH,
        )

    def scale_copy(k):
        return pltpu.make_async_remote_copy(
            stage_s.at[k - 1], arrive_s.at[k - 1], ss_send, ss_recv,
            device_id={"shard": sh_peer(k)}, device_id_type=MESH,
        )

    def to_owners(p):
        rows = slice(p * PR, (p + 1) * PR)

        def stage_step(k, _):
            stage[p, k - 1] = quant[idx_s[k - 1, 0], rows, :]
            if p == 0:
                stage_s[k - 1] = scale[idx_s[k - 1, 0]]
                scale_copy(k).start()
            shard_copy(p, k).start()
            return 0

        lax.fori_loop(1, N_SH, stage_step, 0)
        arrive[p][N_SH - 1] = quant[idx_s[N_SH - 1, 0], rows, :]
        if p == 0:
            arrive_s[N_SH - 1] = scale[idx_s[N_SH - 1, 0]]

    def own_copy(p, k):
        there = z_mate if k == 0 else y_peer(k) * 2 + me_z
        return pltpu.make_async_remote_copy(
            whole.at[p, me_dp], whole.at[p, me_dp], ag_send.at[p, k], ag_recv.at[p, k], **to_dp(there))

    def mate_copy(p, k):
        return pltpu.make_async_remote_copy(
            whole.at[p, z_mate], whole.at[p, z_mate], ag_send.at[p, 3 + k], ag_recv.at[p, 3 + k],
            **to_dp(y_peer(k) * 2 + me_z))

    def gather_scale_copy(k):
        return pltpu.make_async_remote_copy(
            whole_s.at[me_dp], whole_s.at[me_dp], as_send.at[k], as_recv.at[k], **to_dp(dp_peer(k)))

    def pack(p):
        wait_bytes(arrive[p].at[pl.ds(0, N_SH - 1)], sh_recv.at[p])
        for i in range(NT):
            whole[p, me_dp, i] = arrive[p][idx_s[N_SH + i, 0]]
        for k in (0, 1, 3, 2):
            own_copy(p, k).start()

    def pass_on(p):
        own_copy(p, 0).wait_recv()
        for k in (1, 3, 2):
            mate_copy(p, k).start()

    for p in range(AHEAD):
        to_owners(p)
    for p in range(PIECES):
        pack(p)
        if p + AHEAD < PIECES:
            to_owners(p + AHEAD)
        if p == 0:
            wait_bytes(arrive_s.at[pl.ds(0, N_SH - 1)], ss_recv)
            for i in range(NT):
                whole_s[me_dp, i] = arrive_s[idx_s[N_SH + i, 0]]
            for k in range(1, N_DP):
                gather_scale_copy(k).start()
        else:
            pass_on(p - 1)
    pass_on(PIECES - 1)

    for a in range(NZ):
        z1_copy(a).wait_send()
        for k in range(1, 4):
            z2_copy(a, k).wait_send()
    for b in range(NY):
        y2_copy(b).wait_send()
        for k in range(1, 4):
            y1_copy(b, k).wait_send()
    wait_bytes(stage_s.at[pl.ds(0, N_SH - 1)], ss_send)
    for p in range(PIECES):
        wait_bytes(stage.at[p, pl.ds(0, N_SH - 1)], sh_send.at[p])
        own_copy(p, 0).wait_send()
        for k in range(1, 4):
            own_copy(p, k).wait()
            mate_copy(p, k).wait()
    for k in range(1, N_DP):
        gather_scale_copy(k).wait()


def place_kernel(whole, whole_s, place, master_v, moment_v, second_v, tiles, scales, master_out, moment_out, second_out, sem, tile_sem):
    copies = [
        pltpu.make_async_copy(a, b, sem.at[i])
        for i, (a, b) in enumerate(((master_v, master_out), (moment_v, moment_out), (second_v, second_out)))
    ]

    def start(s, _):
        pltpu.make_async_copy(whole.at[:, place[s, 0]], tiles.at[s], tile_sem).start()
        return 0

    lax.fori_loop(0, OWNED, start, 0)
    for copy in copies:
        copy.start()
    lane = lax.broadcasted_iota(jnp.int32, (1, TB), 1)

    def collect(s, acc):
        return jnp.where(lane == s, whole_s[place[s, 0]], acc)

    row = lax.fori_loop(0, OWNED, collect, jnp.zeros((1, TB), jnp.float32))
    scales[...] = row.astype(jnp.bfloat16)
    wait_bytes(tiles, tile_sem)
    for copy in copies:
        copy.wait()


def per_device(gradients, tile_table, master, moment, second):
    shape = master.shape
    flat = (NT * TB, TB)
    f32, bf16 = jnp.float32, jnp.bfloat16
    anywhere = pl.BlockSpec(memory_space=pltpu.HBM)
    vmem = pl.BlockSpec(memory_space=pltpu.VMEM)
    smem = pl.BlockSpec(memory_space=pltpu.SMEM)
    dma = pltpu.SemaphoreType.DMA
    state = jax.ShapeDtypeStruct(flat, f32)
    tile = (TB, TB)
    outs = pl.pallas_call(
        main_kernel,
        out_shape=(
            pltpu.VMEM(flat, f32), pltpu.VMEM(flat, f32), pltpu.VMEM(flat, f32),
            pltpu.VMEM((PIECES, N_DP, NT, PR, TB), bf16),
            pltpu.VMEM((N_DP, NT, 1, TB), f32),
            pltpu.VMEM((OWNED, TB), jnp.int32),
        ),
        in_specs=[anywhere, vmem, anywhere, anywhere, anywhere],
        out_specs=(vmem,) * 6,
        scratch_shapes=[
            pltpu.VMEM((N_DP, NT * TB * TB), bf16),
            pltpu.VMEM((TB, TB), f32),
            pltpu.VMEM((2, NZ, 4) + tile, bf16),
            pltpu.VMEM((NZ, 4) + tile, bf16),
            pltpu.VMEM((NZ, 3) + tile, bf16),
            pltpu.VMEM((NZ, 3) + tile, bf16),
            pltpu.VMEM((NY, 4, 2) + tile, bf16),
            pltpu.VMEM((NY, 3, 2) + tile, bf16),
            pltpu.VMEM((NY,) + tile, bf16),
            pltpu.VMEM((NY,) + tile, bf16),
            pltpu.VMEM(flat, f32), pltpu.VMEM(flat, f32), pltpu.VMEM(flat, f32),
            pltpu.VMEM((NT,) + tile, bf16),
            pltpu.VMEM((NT, 1, TB), f32),
            pltpu.VMEM((PIECES, N_SH, PR, TB), bf16),
            pltpu.VMEM((N_SH, 1, TB), f32),
            pltpu.VMEM((N_SH, 1, TB), f32),
            pltpu.VMEM((48, TB), jnp.int32),
            pltpu.SMEM((48, TB), jnp.int32),
            *[pltpu.VMEM((N_SH, PR, TB), bf16) for _ in range(PIECES)],
            dma((NT,)), dma((3,)), dma(()),
            *[dma((NZ,))] * 4, *[dma((NY,))] * 4,
            dma((PIECES,)), dma((PIECES,)),
            dma(()), dma(()),
            dma((PIECES, 7)), dma((PIECES, 7)),
            dma((N_DP,)), dma((N_DP,)),
        ],
        compiler_params=pltpu.CompilerParams(collective_id=0, has_side_effects=True, vmem_limit_bytes=58 << 20),
    )(
        gradients.reshape(N_DP, NT * TB * TB), tile_table,
        master.reshape(flat), moment.reshape(flat), second.reshape(flat),
    )
    master_new, moment_new, second_new, whole, whole_s, place = outs
    tiles, scales, master_new, moment_new, second_new = pl.pallas_call(
        place_kernel,
        out_shape=(
            jax.ShapeDtypeStruct((OWNED, PIECES, PR, TB), bf16),
            jax.ShapeDtypeStruct((1, TB), bf16),
            state, state, state,
        ),
        in_specs=[vmem, vmem, smem, vmem, vmem, vmem],
        out_specs=(anywhere, vmem, anywhere, anywhere, anywhere),
        scratch_shapes=[dma((3,)), dma(())],
        compiler_params=pltpu.CompilerParams(vmem_limit_bytes=16 << 20),
    )(whole.reshape(PIECES, OWNED, PR, TB), whole_s.reshape(OWNED, 1, TB), place, master_new, moment_new, second_new)
    return (
        master_new.reshape(shape), moment_new.reshape(shape), second_new.reshape(shape),
        tiles.reshape(OWNED, TB, TB), scales[0, :OWNED],
    )


def solution(mesh):
    in_specs = (
        P("dp", "shard", None, None),
        P(),
        P("shard", "dp", None),
        P("shard", "dp", None),
        P("shard", "dp", None),
    )
    out_specs = (
        P("shard", "dp", None),
        P("shard", "dp", None),
        P("shard", "dp", None),
        P("shard", None, None),
        P("shard"),
    )
    return jax.shard_map(
        per_device, mesh=mesh, in_specs=in_specs, out_specs=out_specs, check_vma=False
    )
```

```python
import functools

import jax
import jax.numpy as jnp
from jax import lax
from jax.experimental import pallas as pl
from jax.experimental.pallas import tpu as pltpu
from jax.sharding import PartitionSpec as P

TB = 128
beta_first = 0.9
beta_second = 0.95
learning_rate = 0.002
weight_decay = 0.1
adam_epsilon = 1e-08
scale_epsilon = 1e-06
step_count = 10

MESH = pl.DeviceIdType.MESH
N_DP = 8
N_SH = 32
NT = 12
OWNED = 96
NZ = 5
NY = NT - NZ
HALF = TB // 2
PIECES = 8
AHEAD = 3
PR = TB // PIECES


def wait_bytes(ref, sem):
    pltpu.make_async_copy(ref, ref, sem).wait()


def lane_sum(x):
    return jnp.sum(x, axis=1, keepdims=True)


def index_tables(tab_ref, idx_ref, place_ref, me_sh, me_dp):
    def iota(shape, dim):
        return lax.broadcasted_iota(jnp.int32, shape, dim)

    lane32 = iota((N_SH, OWNED), 1)
    row32 = iota((N_SH, OWNED), 0)
    mine = tab_ref[pl.ds(me_sh, 1), :]
    owner = ((mine >> 5) * 171) >> 9
    offset = jnp.broadcast_to((owner - me_sh - 1) & (N_SH - 1), (N_SH, OWNED))
    col = lane32 - me_dp * NT
    hit = (offset == row32) & (col >= 0) & (col < NT)
    idx_ref[0:N_SH, :] = jnp.broadcast_to(jnp.minimum(lane_sum(jnp.where(hit, col, 0)), NT - 1), (N_SH, TB))

    slot = iota((OWNED, OWNED), 0)
    lane = iota((OWNED, OWNED), 1)
    wanted = slot + me_sh * OWNED

    def find(j, acc):
        row = jnp.broadcast_to(tab_ref[pl.ds(j, 1), :], (OWNED, OWNED))
        return acc + jnp.where(row == wanted, lane + j * TB, 0)

    found = lane_sum(lax.fori_loop(0, N_SH, find, jnp.zeros((OWNED, OWNED), jnp.int32)))
    found = jnp.broadcast_to(found, (OWNED, OWNED))
    source = found >> 7
    part = ((found & (TB - 1)) * 43) >> 9

    def as_row(x):
        return jnp.sum(jnp.where(slot == lane, x, 0), axis=0, keepdims=True)

    part_row = jnp.broadcast_to(as_row(part), (OWNED, OWNED))
    rank = lane_sum(jnp.where((part_row == part) & (lane < slot), 1, 0))
    rank = jnp.broadcast_to(rank, (OWNED, OWNED))
    place_ref[...] = jnp.broadcast_to(jnp.clip(part * NT + rank, 0, OWNED - 1)[:, 0:1], (OWNED, TB))
    arrival = as_row((me_sh - source - 1) & (N_SH - 1))
    key = as_row(jnp.where(part == me_dp, rank, -1))
    row16 = iota((16, OWNED), 0)
    pick = jnp.where(jnp.broadcast_to(key, (16, OWNED)) == row16, jnp.broadcast_to(arrival, (16, OWNED)), 0)
    idx_ref[N_SH : N_SH + 16, :] = jnp.broadcast_to(lane_sum(pick) & (N_SH - 1), (16, TB))


def adam(grad, master, moment, second):
    moment_new = beta_first * moment + (1.0 - beta_first) * grad
    second_new = beta_second * second + (1.0 - beta_second) * grad * grad
    first_fix = 1.0 - beta_first**step_count
    second_fix = 1.0 - beta_second**step_count
    update = moment_new / first_fix / (jnp.sqrt(second_new / second_fix) + adam_epsilon)
    master_new = master - learning_rate * (update + weight_decay * master)
    return master_new, moment_new, second_new


def main_kernel(
    g_hbm, tab_ref, master_hbm, moment_hbm, second_hbm,
    master_out, moment_out, second_out, whole, whole_s, place,
    g_v, spread, z_own, z_got, z_part, z_relay, z_sum, z_last,
    y_own, y_relay, y_sum, y_got, y_part, y_last,
    master_v, moment_v, second_v, quant, scale, stage, stage_s, arrive_s, idx_v, idx_s, *rest,
):
    arrive = rest[:PIECES]
    (
        in_sem, st_sem, idx_sem,
        z1_send, z1_recv, zr_send, zr_recv, zo_send, zs_send, zf_recv,
        yr_send, yr_recv, yo_send, ys_send, yf_recv, y2_send, y2_recv,
        sh_send, sh_recv, ss_send, ss_recv, ag_send, ag_recv, as_send, as_recv, greet,
    ) = rest[PIECES:]
    me_dp = lax.axis_index("dp")
    me_sh = lax.axis_index("shard")
    me_y, me_z = me_dp // 2, me_dp % 2
    me_x, me_h, me_c = me_sh // 8, (me_sh // 2) % 4, me_sh % 2

    def dp_peer(k):
        return lax.rem(me_dp + k, N_DP)

    def sh_peer(k):
        return lax.rem(me_sh + k, N_SH)

    def y_peer(k):
        return lax.rem(me_y + k, 4)

    def to_dp(d):
        return dict(device_id={"dp": d}, device_id_type=MESH)

    def to_y(k):
        return to_dp(y_peer(k) * 2 + me_z)

    z_mate = me_y * 2 + 1 - me_z
    core_mate = {"shard": me_sh + 1 - 2 * me_c}
    x_next = [{"shard": lax.rem(me_x + k, 4) * 8 + me_h * 2 + me_c} for k in (1, 3)]
    h_next = [{"shard": me_x * 8 + lax.rem(me_h + k, 4) * 2 + me_c} for k in (1, 3)]
    cols = TB * TB
    f32, bf16 = jnp.float32, jnp.bfloat16
    NEXT, OPPOSITE, PREVIOUS = 1, 2, 3
    FIRST, SECOND = slice(0, HALF), slice(HALF, TB)

    order = []
    for i in range(max(NZ, NY)):
        order += [("y", i)] * (i < NY) + [("z", i)] * (i < NZ)

    def tile_of(item):
        return item[1] + (NZ if item[0] == "y" else 0)

    def load_gradient(t):
        at = pl.ds(t * cols, cols)
        return pltpu.make_async_copy(g_hbm.at[:, at], g_v.at[:, at], in_sem.at[t])

    barrier = pltpu.get_barrier_semaphore()
    near = [{"dp": z_mate}] + [{"dp": y_peer(k) * 2 + me_z} for k in (1, 2, 3)] + [core_mate] + x_next + h_next
    for device in near:
        pl.semaphore_signal(barrier, 1, device_id=device, device_id_type=MESH)
    for item in order:
        load_gradient(tile_of(item)).start()
    states = [
        pltpu.make_async_copy(a, b, st_sem.at[i])
        for i, (a, b) in enumerate(((master_hbm, master_v), (moment_hbm, moment_v), (second_hbm, second_v)))
    ]
    for copy in states:
        copy.start()

    def greetings(stage, devices):
        for device in devices:
            pl.semaphore_signal(greet.at[stage], 1, device_id=device, device_id_type=MESH)

    def greeted(stage, count):
        pl.semaphore_wait(greet.at[stage], count)

    def split_rows(item):
        t = tile_of(item)
        load_gradient(t).wait()

        def group(c, _):
            at = pl.multiple_of(t * cols + c * 2048, 2048)
            for u in range(16):
                spread[u * 8 : u * 8 + 8, :] = g_v[:, pl.ds(at + u * TB, TB)].astype(f32)
            rows = pl.ds(pl.multiple_of(c * 16, 16), 16)
            for i in range(N_DP):
                value = spread[pl.ds(i, 16, stride=8), :].astype(bf16)
                if item[0] == "z":
                    z_own[i % 2, item[1], i // 2, rows, :] = value
                else:
                    y_own[item[1], i // 2, i % 2, rows, :] = value
            return 0

        lax.fori_loop(0, 8, group, 0)

    def remote(src, dst, send, recv, there):
        return pltpu.make_async_remote_copy(src, dst, send, recv, **there)

    def z1_copy(a):
        return remote(z_own.at[1 - me_z, a], z_got.at[a], z1_send.at[a], z1_recv.at[a], to_dp(z_mate))

    def z_relays(a):
        return [
            remote(z_part.at[a, OPPOSITE - 1, FIRST], z_relay.at[a, 0], zr_send.at[a], zr_recv.at[a, 0], to_y(NEXT)),
            remote(z_part.at[a, OPPOSITE - 1, SECOND], z_relay.at[a, 1], zr_send.at[a], zr_recv.at[a, 1], to_y(PREVIOUS)),
        ]

    def z_owns(a):
        return [
            remote(z_part.at[a, NEXT - 1, SECOND], z_last.at[a, 0, SECOND], zo_send.at[a], zf_recv.at[a], to_y(NEXT)),
            remote(z_part.at[a, PREVIOUS - 1, FIRST], z_last.at[a, 1, FIRST], zo_send.at[a], zf_recv.at[a], to_y(PREVIOUS)),
        ]

    def z_sums(a):
        return [
            remote(z_sum.at[a, 0], z_last.at[a, 0, FIRST], zs_send.at[a], zf_recv.at[a], to_y(NEXT)),
            remote(z_sum.at[a, 1], z_last.at[a, 1, SECOND], zs_send.at[a], zf_recv.at[a], to_y(PREVIOUS)),
        ]

    def y_relays(b):
        opposite = y_peer(OPPOSITE)
        return [
            remote(y_own.at[b, opposite, :, FIRST], y_relay.at[b, 0], yr_send.at[b], yr_recv.at[b, 0], to_y(NEXT)),
            remote(y_own.at[b, opposite, :, SECOND], y_relay.at[b, 1], yr_send.at[b], yr_recv.at[b, 1], to_y(PREVIOUS)),
        ]

    def y_owns(b):
        return [
            remote(y_own.at[b, y_peer(NEXT), :, SECOND], y_got.at[b, 0, :, SECOND], yo_send.at[b], yf_recv.at[b], to_y(NEXT)),
            remote(y_own.at[b, y_peer(PREVIOUS), :, FIRST], y_got.at[b, 1, :, FIRST], yo_send.at[b], yf_recv.at[b], to_y(PREVIOUS)),
        ]

    def y_sums(b):
        return [
            remote(y_sum.at[b, 0], y_got.at[b, 0, :, FIRST], ys_send.at[b], yf_recv.at[b], to_y(NEXT)),
            remote(y_sum.at[b, 1], y_got.at[b, 1, :, SECOND], ys_send.at[b], yf_recv.at[b], to_y(PREVIOUS)),
        ]

    def y2_copy(b):
        return remote(y_part.at[b], y_last.at[b], y2_send.at[b], y2_recv.at[b], to_dp(z_mate))

    def start(copies):
        for copy in copies:
            copy.start()

    def first_sends(item):
        if item[0] == "z":
            z1_copy(item[1]).start()
        else:
            start(y_relays(item[1]) + y_owns(item[1]))

    split_rows(order[0])
    pl.semaphore_wait(barrier, len(near))
    first_sends(order[0])
    greetings(0, x_next)
    for n, item in enumerate(order[1:]):
        split_rows(item)
        first_sends(item)
        if n == 2:
            greeted(0, 2)
            greetings(1, h_next)
        if n == 4:
            greeted(1, 2)
            greetings(2, h_next)
        if n == 6:
            greeted(2, 2)
            greetings(3, [core_mate])
        if n == 7:
            greeted(3, 1)

    def blocks(body, init=0, rows=TB):
        return lax.fori_loop(0, rows // 32, lambda b, c: body(pl.multiple_of(b * 32, 32), c), init)

    def relay(item):
        i = item[1]
        if item[0] == "z":
            for side, copy in enumerate(z_relays(i)):
                copy.wait_recv()

            def add(b, _):
                one, two = pl.ds(b, 32), pl.ds(b + HALF, 32)
                z_sum[i, 0, one, :] = (z_part[i, NEXT - 1, one, :].astype(f32) + z_relay[i, 0, one, :].astype(f32)).astype(bf16)
                z_sum[i, 1, one, :] = (z_part[i, PREVIOUS - 1, two, :].astype(f32) + z_relay[i, 1, one, :].astype(f32)).astype(bf16)
                return 0

            blocks(add, rows=HALF)
            start(z_sums(i))
        else:
            for side, copy in enumerate(y_relays(i)):
                copy.wait_recv()

            def add(b, _):
                one, two = pl.ds(b, 32), pl.ds(b + HALF, 32)
                for z in range(2):
                    y_sum[i, 0, z, one, :] = (y_own[i, y_peer(NEXT), z, one, :].astype(f32) + y_relay[i, 0, z, one, :].astype(f32)).astype(bf16)
                    y_sum[i, 1, z, one, :] = (y_own[i, y_peer(PREVIOUS), z, two, :].astype(f32) + y_relay[i, 1, z, one, :].astype(f32)).astype(bf16)
                return 0

            blocks(add, rows=HALF)
            start(y_sums(i))

    def middle(item):
        i = item[1]
        if item[0] == "z":
            z1_copy(i).wait_recv()

            def add(b, _):
                rows = pl.ds(b, 32)
                for k in (OPPOSITE, NEXT, PREVIOUS):
                    y = y_peer(k)
                    z_part[i, k - 1, rows, :] = (
                        z_own[me_z, i, y, rows, :].astype(f32) + z_got[i, y, rows, :].astype(f32)
                    ).astype(bf16)
                return 0

            blocks(add)
            start(z_relays(i) + z_owns(i))
        else:
            wait_bytes(y_got.at[i], yf_recv.at[i])

            def add(b, _):
                rows = pl.ds(b, 32)
                other = y_own[i, me_y, 1 - me_z, rows, :].astype(f32)
                for k in range(2):
                    other = other + y_got[i, k, 1 - me_z, rows, :].astype(f32)
                y_part[i, rows, :] = other.astype(bf16)
                return 0

            blocks(add)
            y2_copy(i).start()

    def last(item):
        i, t = item[1], tile_of(item)
        if item[0] == "z":
            wait_bytes(z_last.at[i], zf_recv.at[i])
        else:
            y2_copy(i).wait_recv()

        def step(b, largest):
            rows = pl.ds(b, 32)
            flat = pl.ds(t * TB + b, 32)
            if item[0] == "z":
                terms = [z_own[me_z, i, me_y, rows, :], z_got[i, me_y, rows, :]]
                terms += [z_last[i, k, rows, :] for k in range(2)]
            else:
                terms = [y_own[i, me_y, me_z, rows, :]] + [y_got[i, k, me_z, rows, :] for k in range(2)]
                terms += [y_last[i, rows, :]]
            grad = functools.reduce(lambda a, b: a + b, [x.astype(f32) for x in terms])
            new = adam(grad, master_v[flat, :], moment_v[flat, :], second_v[flat, :])
            master_out[flat, :], moment_out[flat, :], second_out[flat, :] = new
            return jnp.maximum(largest, jnp.abs(new[0]))

        largest = blocks(step, jnp.zeros((32, TB), f32))
        largest = jnp.max(jnp.max(largest, axis=0, keepdims=True), axis=1, keepdims=True)
        tile_scale = (jnp.broadcast_to(largest, (16, TB)) + scale_epsilon).astype(bf16).astype(f32)
        scale[t] = tile_scale[0:1, :]
        divisor = jnp.broadcast_to(tile_scale[0:1, :], (TB, TB))
        quant[t] = (master_out[t * TB : (t + 1) * TB, :] / divisor).astype(bf16)

    acts = {"r": relay, "m": middle, "l": last}
    steps = (
        "ry0 mz0 ry1 mz1 ry2 mz2 ry3 ry4 mz3 tables ry5 rz0 my0 ry6 rz1 my1 mz4 rz2 my2 my3 rz3 my4 states "
        "lz0 my5 lz1 rz4 my6 lz2 ly0 ly1 lz3 ly2 ly3 lz4 ly4 ly5 ly6"
    )
    for step in steps.split():
        if step == "tables":
            index_tables(tab_ref, idx_v, place, me_sh, me_dp)
            idx_copy = pltpu.make_async_copy(idx_v, idx_s, idx_sem)
            idx_copy.start()
        elif step == "states":
            idx_copy.wait()
            for copy in states:
                copy.wait()
        else:
            acts[step[0]]((step[1], int(step[2:])))

    def shard_copy(p, k):
        return remote(stage.at[p, k - 1], arrive[p].at[k - 1], sh_send.at[p], sh_recv.at[p],
                      dict(device_id={"shard": sh_peer(k)}, device_id_type=MESH))

    def scale_copy(k):
        return remote(stage_s.at[k - 1], arrive_s.at[k - 1], ss_send, ss_recv,
                      dict(device_id={"shard": sh_peer(k)}, device_id_type=MESH))

    def to_owners(p):
        rows = slice(p * PR, (p + 1) * PR)

        def stage_step(k, _):
            stage[p, k - 1] = quant[idx_s[k - 1, 0], rows, :]
            if p == 0:
                stage_s[k - 1] = scale[idx_s[k - 1, 0]]
                scale_copy(k).start()
            shard_copy(p, k).start()
            return 0

        lax.fori_loop(1, N_SH, stage_step, 0)
        arrive[p][N_SH - 1] = quant[idx_s[N_SH - 1, 0], rows, :]
        if p == 0:
            arrive_s[N_SH - 1] = scale[idx_s[N_SH - 1, 0]]

    def block_copy(p, d, n, there):
        return remote(whole.at[p, d], whole.at[p, d], ag_send.at[p, n], ag_recv.at[p, n], there)

    def mate_of(k):
        return y_peer(k) * 2 + 1 - me_z

    def same_of(k):
        return y_peer(k) * 2 + me_z

    def own_copies(p):
        return [block_copy(p, me_dp, 0, to_dp(z_mate)), block_copy(p, me_dp, 1, to_y(NEXT)), block_copy(p, me_dp, 2, to_y(PREVIOUS))]

    def mate_copies(p):
        return [block_copy(p, z_mate, 3, to_y(NEXT)), block_copy(p, z_mate, 4, to_y(PREVIOUS))]

    def on_copies(p):
        return [block_copy(p, same_of(PREVIOUS), 5, to_y(NEXT)), block_copy(p, mate_of(NEXT), 6, to_y(PREVIOUS))]

    def gather_scale_copy(k):
        return remote(whole_s.at[me_dp], whole_s.at[me_dp], as_send.at[k], as_recv.at[k], to_dp(dp_peer(k)))

    def pack(p):
        wait_bytes(arrive[p].at[pl.ds(0, N_SH - 1)], sh_recv.at[p])
        for i in range(NT):
            whole[p, me_dp, i] = arrive[p][idx_s[N_SH + i, 0]]
        start(own_copies(p))

    def pass_mate(p):
        own_copies(p)[0].wait_recv()
        start(mate_copies(p))

    def pass_same(p):
        own_copies(p)[1].wait_recv()
        on_copies(p)[0].start()

    def pass_other(p):
        mate_copies(p)[1].wait_recv()
        on_copies(p)[1].start()

    for p in range(AHEAD):
        to_owners(p)
    for p in range(PIECES + 2):
        if p < PIECES:
            pack(p)
        if p + AHEAD < PIECES:
            to_owners(p + AHEAD)
        if p == 0:
            wait_bytes(arrive_s.at[pl.ds(0, N_SH - 1)], ss_recv)
            for i in range(NT):
                whole_s[me_dp, i] = arrive_s[idx_s[N_SH + i, 0]]
            for k in range(1, N_DP):
                gather_scale_copy(k).start()
        if 0 <= p - 1 < PIECES:
            pass_mate(p - 1)
            pass_same(p - 1)
        if 0 <= p - 2 < PIECES:
            pass_other(p - 2)

    for a in range(NZ):
        for copy in [z1_copy(a)] + z_relays(a) + z_owns(a) + z_sums(a):
            copy.wait_send()
    for b in range(NY):
        for copy in [y2_copy(b)] + y_relays(b) + y_owns(b) + y_sums(b):
            copy.wait_send()
    wait_bytes(stage_s.at[pl.ds(0, N_SH - 1)], ss_send)
    for p in range(PIECES):
        wait_bytes(stage.at[p, pl.ds(0, N_SH - 1)], sh_send.at[p])
        own, mate, on = own_copies(p), mate_copies(p), on_copies(p)
        for copy in own + mate + on:
            copy.wait_send()
        for copy in [own[2], mate[0]] + on:
            copy.wait_recv()
    for k in range(1, N_DP):
        gather_scale_copy(k).wait()


def place_kernel(whole, whole_s, place, master_v, moment_v, second_v, tiles, scales, master_out, moment_out, second_out, sem, tile_sem):
    copies = [
        pltpu.make_async_copy(a, b, sem.at[i])
        for i, (a, b) in enumerate(((master_v, master_out), (moment_v, moment_out), (second_v, second_out)))
    ]

    def start(s, _):
        pltpu.make_async_copy(whole.at[:, place[s, 0]], tiles.at[s], tile_sem).start()
        return 0

    lax.fori_loop(0, OWNED, start, 0)
    for copy in copies:
        copy.start()
    lane = lax.broadcasted_iota(jnp.int32, (1, TB), 1)

    def collect(s, acc):
        return jnp.where(lane == s, whole_s[place[s, 0]], acc)

    row = lax.fori_loop(0, OWNED, collect, jnp.zeros((1, TB), jnp.float32))
    scales[...] = row.astype(jnp.bfloat16)
    wait_bytes(tiles, tile_sem)
    for copy in copies:
        copy.wait()


def per_device(gradients, tile_table, master, moment, second):
    shape = master.shape
    flat = (NT * TB, TB)
    f32, bf16 = jnp.float32, jnp.bfloat16
    anywhere = pl.BlockSpec(memory_space=pltpu.HBM)
    vmem = pl.BlockSpec(memory_space=pltpu.VMEM)
    smem = pl.BlockSpec(memory_space=pltpu.SMEM)
    dma = pltpu.SemaphoreType.DMA
    state = jax.ShapeDtypeStruct(flat, f32)
    tile, half = (TB, TB), (HALF, TB)
    outs = pl.pallas_call(
        main_kernel,
        out_shape=(
            pltpu.VMEM(flat, f32), pltpu.VMEM(flat, f32), pltpu.VMEM(flat, f32),
            pltpu.VMEM((PIECES, N_DP, NT, PR, TB), bf16),
            pltpu.VMEM((N_DP, NT, 1, TB), f32),
            pltpu.VMEM((OWNED, TB), jnp.int32),
        ),
        in_specs=[anywhere, vmem, anywhere, anywhere, anywhere],
        out_specs=(vmem,) * 6,
        scratch_shapes=[
            pltpu.VMEM((N_DP, NT * TB * TB), bf16),
            pltpu.VMEM((TB, TB), f32),
            pltpu.VMEM((2, NZ, 4) + tile, bf16),
            pltpu.VMEM((NZ, 4) + tile, bf16),
            pltpu.VMEM((NZ, 3) + tile, bf16),
            pltpu.VMEM((NZ, 2) + half, bf16),
            pltpu.VMEM((NZ, 2) + half, bf16),
            pltpu.VMEM((NZ, 2) + tile, bf16),
            pltpu.VMEM((NY, 4, 2) + tile, bf16),
            pltpu.VMEM((NY, 2, 2) + half, bf16),
            pltpu.VMEM((NY, 2, 2) + half, bf16),
            pltpu.VMEM((NY, 2, 2) + tile, bf16),
            pltpu.VMEM((NY,) + tile, bf16),
            pltpu.VMEM((NY,) + tile, bf16),
            pltpu.VMEM(flat, f32), pltpu.VMEM(flat, f32), pltpu.VMEM(flat, f32),
            pltpu.VMEM((NT,) + tile, bf16),
            pltpu.VMEM((NT, 1, TB), f32),
            pltpu.VMEM((PIECES, N_SH, PR, TB), bf16),
            pltpu.VMEM((N_SH, 1, TB), f32),
            pltpu.VMEM((N_SH, 1, TB), f32),
            pltpu.VMEM((48, TB), jnp.int32),
            pltpu.SMEM((48, TB), jnp.int32),
            *[pltpu.VMEM((N_SH, PR, TB), bf16) for _ in range(PIECES)],
            dma((NT,)), dma((3,)), dma(()),
            dma((NZ,)), dma((NZ,)), dma((NZ,)), dma((NZ, 2)), dma((NZ,)), dma((NZ,)), dma((NZ,)),
            dma((NY,)), dma((NY, 2)), dma((NY,)), dma((NY,)), dma((NY,)), dma((NY,)), dma((NY,)),
            dma((PIECES,)), dma((PIECES,)),
            dma(()), dma(()),
            dma((PIECES, 7)), dma((PIECES, 7)),
            dma((N_DP,)), dma((N_DP,)),
            pltpu.SemaphoreType.REGULAR((4,)),
        ],
        compiler_params=pltpu.CompilerParams(collective_id=0, has_side_effects=True, vmem_limit_bytes=58 << 20),
    )(
        gradients.reshape(N_DP, NT * TB * TB), tile_table,
        master.reshape(flat), moment.reshape(flat), second.reshape(flat),
    )
    master_new, moment_new, second_new, whole, whole_s, place = outs
    tiles, scales, master_new, moment_new, second_new = pl.pallas_call(
        place_kernel,
        out_shape=(
            jax.ShapeDtypeStruct((OWNED, PIECES, PR, TB), bf16),
            jax.ShapeDtypeStruct((1, TB), bf16),
            state, state, state,
        ),
        in_specs=[vmem, vmem, smem, vmem, vmem, vmem],
        out_specs=(anywhere, vmem, anywhere, anywhere, anywhere),
        scratch_shapes=[dma((3,)), dma(())],
        compiler_params=pltpu.CompilerParams(vmem_limit_bytes=16 << 20),
    )(whole.reshape(PIECES, OWNED, PR, TB), whole_s.reshape(OWNED, 1, TB), place, master_new, moment_new, second_new)
    return (
        master_new.reshape(shape), moment_new.reshape(shape), second_new.reshape(shape),
        tiles.reshape(OWNED, TB, TB), scales[0, :OWNED],
    )


def solution(mesh):
    in_specs = (
        P("dp", "shard", None, None),
        P(),
        P("shard", "dp", None),
        P("shard", "dp", None),
        P("shard", "dp", None),
    )
    out_specs = (
        P("shard", "dp", None),
        P("shard", "dp", None),
        P("shard", "dp", None),
        P("shard", None, None),
        P("shard"),
    )
    return jax.shard_map(
        per_device, mesh=mesh, in_specs=in_specs, out_specs=out_specs, check_vma=False
    )
```

```python
import functools

import jax
import jax.numpy as jnp
from jax import lax
from jax.experimental import pallas as pl
from jax.experimental.pallas import tpu as pltpu
from jax.sharding import PartitionSpec as P

TB = 128
beta_first = 0.9
beta_second = 0.95
learning_rate = 0.002
weight_decay = 0.1
adam_epsilon = 1e-08
scale_epsilon = 1e-06
step_count = 10

MESH = pl.DeviceIdType.MESH
N_DP = 8
N_SH = 32
NT = 12
OWNED = 96
NZ = 5
NY = NT - NZ
HALF = TB // 2
PIECES = 8
AHEAD = 3
PR = TB // PIECES


def wait_bytes(ref, sem):
    pltpu.make_async_copy(ref, ref, sem).wait()


def lane_sum(x):
    return jnp.sum(x, axis=1, keepdims=True)


def index_tables(tab_ref, idx_ref, place_ref, me_sh, me_dp):
    def iota(shape, dim):
        return lax.broadcasted_iota(jnp.int32, shape, dim)

    lane32 = iota((N_SH, OWNED), 1)
    row32 = iota((N_SH, OWNED), 0)
    mine = tab_ref[pl.ds(me_sh, 1), :]
    owner = ((mine >> 5) * 171) >> 9
    offset = jnp.broadcast_to((owner - me_sh - 1) & (N_SH - 1), (N_SH, OWNED))
    col = lane32 - me_dp * NT
    hit = (offset == row32) & (col >= 0) & (col < NT)
    idx_ref[0:N_SH, :] = jnp.broadcast_to(jnp.minimum(lane_sum(jnp.where(hit, col, 0)), NT - 1), (N_SH, TB))

    slot = iota((OWNED, OWNED), 0)
    lane = iota((OWNED, OWNED), 1)
    wanted = slot + me_sh * OWNED

    def find(j, acc):
        row = jnp.broadcast_to(tab_ref[pl.ds(j, 1), :], (OWNED, OWNED))
        return acc + jnp.where(row == wanted, lane + j * TB, 0)

    found = lane_sum(lax.fori_loop(0, N_SH, find, jnp.zeros((OWNED, OWNED), jnp.int32)))
    found = jnp.broadcast_to(found, (OWNED, OWNED))
    source = found >> 7
    part = ((found & (TB - 1)) * 43) >> 9

    def as_row(x):
        return jnp.sum(jnp.where(slot == lane, x, 0), axis=0, keepdims=True)

    part_row = jnp.broadcast_to(as_row(part), (OWNED, OWNED))
    rank = lane_sum(jnp.where((part_row == part) & (lane < slot), 1, 0))
    rank = jnp.broadcast_to(rank, (OWNED, OWNED))
    place_ref[...] = jnp.broadcast_to(jnp.clip(part * NT + rank, 0, OWNED - 1)[:, 0:1], (OWNED, TB))
    arrival = as_row((me_sh - source - 1) & (N_SH - 1))
    key = as_row(jnp.where(part == me_dp, rank, -1))
    row16 = iota((16, OWNED), 0)
    pick = jnp.where(jnp.broadcast_to(key, (16, OWNED)) == row16, jnp.broadcast_to(arrival, (16, OWNED)), 0)
    idx_ref[N_SH : N_SH + 16, :] = jnp.broadcast_to(lane_sum(pick) & (N_SH - 1), (16, TB))


def adam(grad, master, moment, second):
    moment_new = beta_first * moment + (1.0 - beta_first) * grad
    second_new = beta_second * second + (1.0 - beta_second) * grad * grad
    first_fix = 1.0 - beta_first**step_count
    second_fix = 1.0 - beta_second**step_count
    update = moment_new / first_fix / (jnp.sqrt(second_new / second_fix) + adam_epsilon)
    master_new = master - learning_rate * (update + weight_decay * master)
    return master_new, moment_new, second_new


def main_kernel(
    g_hbm, tab_ref, master_hbm, moment_hbm, second_hbm,
    master_out, moment_out, second_out, whole, whole_s, place,
    g_v, spread, z_own, z_got, z_part, z_relay, z_sum, z_last,
    y_own, y_relay, y_sum, y_got, y_part, y_last,
    master_v, moment_v, second_v, quant, scale, stage, stage_s, arrive_s, idx_v, idx_s, *rest,
):
    arrive = rest[:PIECES]
    (
        in_sem, st_sem, idx_sem,
        z1_send, z1_recv, zr_send, zr_recv, zo_send, zs_send, zf_recv,
        yr_send, yr_recv, yo_send, ys_send, yf_recv, y2_send, y2_recv,
        sh_send, sh_recv, ss_send, ss_recv, ag_send, ag_recv, as_send, as_recv, greet,
    ) = rest[PIECES:]
    me_dp = lax.axis_index("dp")
    me_sh = lax.axis_index("shard")
    me_y, me_z = me_dp // 2, me_dp % 2
    me_x, me_h, me_c = me_sh // 8, (me_sh // 2) % 4, me_sh % 2

    def dp_peer(k):
        return lax.rem(me_dp + k, N_DP)

    def sh_peer(k):
        return lax.rem(me_sh + k, N_SH)

    def y_peer(k):
        return lax.rem(me_y + k, 4)

    def to_dp(d):
        return dict(device_id={"dp": d}, device_id_type=MESH)

    def to_y(k):
        return to_dp(y_peer(k) * 2 + me_z)

    z_mate = me_y * 2 + 1 - me_z
    core_mate = {"shard": me_sh + 1 - 2 * me_c}
    x_next = [{"shard": lax.rem(me_x + k, 4) * 8 + me_h * 2 + me_c} for k in (1, 3)]
    h_next = [{"shard": me_x * 8 + lax.rem(me_h + k, 4) * 2 + me_c} for k in (1, 3)]
    cols = TB * TB
    f32, bf16 = jnp.float32, jnp.bfloat16
    NEXT, OPPOSITE, PREVIOUS = 1, 2, 3
    FIRST, SECOND = slice(0, HALF), slice(HALF, TB)

    order = []
    for i in range(max(NZ, NY)):
        order += [("y", i)] * (i < NY) + [("z", i)] * (i < NZ)

    def tile_of(item):
        return item[1] + (NZ if item[0] == "y" else 0)

    def load_gradient(t):
        at = pl.ds(t * cols, cols)
        return pltpu.make_async_copy(g_hbm.at[:, at], g_v.at[:, at], in_sem.at[t])

    barrier = pltpu.get_barrier_semaphore()
    near = [{"dp": z_mate}] + [{"dp": y_peer(k) * 2 + me_z} for k in (1, 2, 3)] + [core_mate] + x_next + h_next
    for device in near:
        pl.semaphore_signal(barrier, 1, device_id=device, device_id_type=MESH)
    for item in order:
        load_gradient(tile_of(item)).start()
    states = [
        pltpu.make_async_copy(a, b, st_sem.at[i])
        for i, (a, b) in enumerate(((master_hbm, master_v), (moment_hbm, moment_v), (second_hbm, second_v)))
    ]
    for copy in states:
        copy.start()

    def greetings(stage, devices):
        for device in devices:
            pl.semaphore_signal(greet.at[stage], 1, device_id=device, device_id_type=MESH)

    def greeted(stage, count):
        pl.semaphore_wait(greet.at[stage], count)

    def split_rows(item):
        t = tile_of(item)
        load_gradient(t).wait()

        def group(c, _):
            at = pl.multiple_of(t * cols + c * 2048, 2048)
            for u in range(16):
                spread[u * 8 : u * 8 + 8, :] = g_v[:, pl.ds(at + u * TB, TB)].astype(f32)
            rows = pl.ds(pl.multiple_of(c * 16, 16), 16)
            for i in range(N_DP):
                value = spread[pl.ds(i, 16, stride=8), :].astype(bf16)
                if item[0] == "z":
                    z_own[i % 2, item[1], i // 2, rows, :] = value
                else:
                    y_own[item[1], i // 2, i % 2, rows, :] = value
            return 0

        lax.fori_loop(0, 8, group, 0)

    def remote(src, dst, send, recv, there):
        return pltpu.make_async_remote_copy(src, dst, send, recv, **there)

    def z1_copy(a):
        return remote(z_own.at[1 - me_z, a], z_got.at[a], z1_send.at[a], z1_recv.at[a], to_dp(z_mate))

    def z_relays(a):
        return [
            remote(z_part.at[a, OPPOSITE - 1, FIRST], z_relay.at[a, 0], zr_send.at[a], zr_recv.at[a, 0], to_y(NEXT)),
            remote(z_part.at[a, OPPOSITE - 1, SECOND], z_relay.at[a, 1], zr_send.at[a], zr_recv.at[a, 1], to_y(PREVIOUS)),
        ]

    def z_owns(a):
        return [
            remote(z_part.at[a, NEXT - 1, SECOND], z_last.at[a, 0, SECOND], zo_send.at[a], zf_recv.at[a], to_y(NEXT)),
            remote(z_part.at[a, PREVIOUS - 1, FIRST], z_last.at[a, 1, FIRST], zo_send.at[a], zf_recv.at[a], to_y(PREVIOUS)),
        ]

    def z_sums(a):
        return [
            remote(z_sum.at[a, 0], z_last.at[a, 0, FIRST], zs_send.at[a], zf_recv.at[a], to_y(NEXT)),
            remote(z_sum.at[a, 1], z_last.at[a, 1, SECOND], zs_send.at[a], zf_recv.at[a], to_y(PREVIOUS)),
        ]

    def y_relays(b):
        opposite = y_peer(OPPOSITE)
        return [
            remote(y_own.at[b, opposite, :, FIRST], y_relay.at[b, 0], yr_send.at[b], yr_recv.at[b, 0], to_y(NEXT)),
            remote(y_own.at[b, opposite, :, SECOND], y_relay.at[b, 1], yr_send.at[b], yr_recv.at[b, 1], to_y(PREVIOUS)),
        ]

    def y_owns(b):
        return [
            remote(y_own.at[b, y_peer(NEXT), :, SECOND], y_got.at[b, 0, :, SECOND], yo_send.at[b], yf_recv.at[b], to_y(NEXT)),
            remote(y_own.at[b, y_peer(PREVIOUS), :, FIRST], y_got.at[b, 1, :, FIRST], yo_send.at[b], yf_recv.at[b], to_y(PREVIOUS)),
        ]

    def y_sums(b):
        return [
            remote(y_sum.at[b, 0], y_got.at[b, 0, :, FIRST], ys_send.at[b], yf_recv.at[b], to_y(NEXT)),
            remote(y_sum.at[b, 1], y_got.at[b, 1, :, SECOND], ys_send.at[b], yf_recv.at[b], to_y(PREVIOUS)),
        ]

    def y2_copy(b):
        return remote(y_part.at[b], y_last.at[b], y2_send.at[b], y2_recv.at[b], to_dp(z_mate))

    def start(copies):
        for copy in copies:
            copy.start()

    def first_sends(item):
        if item[0] == "z":
            z1_copy(item[1]).start()
        else:
            start(y_relays(item[1]) + y_owns(item[1]))

    split_rows(order[0])
    pl.semaphore_wait(barrier, len(near))
    first_sends(order[0])
    greetings(0, x_next)
    for item in order[1:]:
        split_rows(item)
        first_sends(item)

    def blocks(body, init=0, rows=TB):
        return lax.fori_loop(0, rows // 32, lambda b, c: body(pl.multiple_of(b * 32, 32), c), init)

    def relay(item):
        i = item[1]
        if item[0] == "z":
            for copy in z_relays(i):
                copy.wait_recv()

            def add(b, _):
                one, two = pl.ds(b, 32), pl.ds(b + HALF, 32)
                z_sum[i, 0, one, :] = (z_part[i, NEXT - 1, one, :].astype(f32) + z_relay[i, 0, one, :].astype(f32)).astype(bf16)
                z_sum[i, 1, one, :] = (z_part[i, PREVIOUS - 1, two, :].astype(f32) + z_relay[i, 1, one, :].astype(f32)).astype(bf16)
                return 0

            blocks(add, rows=HALF)
            start(z_sums(i))
        else:
            for copy in y_relays(i):
                copy.wait_recv()

            def add(b, _):
                one, two = pl.ds(b, 32), pl.ds(b + HALF, 32)
                for z in range(2):
                    y_sum[i, 0, z, one, :] = (y_own[i, y_peer(NEXT), z, one, :].astype(f32) + y_relay[i, 0, z, one, :].astype(f32)).astype(bf16)
                    y_sum[i, 1, z, one, :] = (y_own[i, y_peer(PREVIOUS), z, two, :].astype(f32) + y_relay[i, 1, z, one, :].astype(f32)).astype(bf16)
                return 0

            blocks(add, rows=HALF)
            start(y_sums(i))

    def middle(item):
        i = item[1]
        if item[0] == "z":
            z1_copy(i).wait_recv()

            def add(b, _):
                rows = pl.ds(b, 32)
                for k in (OPPOSITE, NEXT, PREVIOUS):
                    y = y_peer(k)
                    z_part[i, k - 1, rows, :] = (
                        z_own[me_z, i, y, rows, :].astype(f32) + z_got[i, y, rows, :].astype(f32)
                    ).astype(bf16)
                return 0

            blocks(add)
            start(z_relays(i) + z_owns(i))
        else:
            wait_bytes(y_got.at[i], yf_recv.at[i])

            def add(b, _):
                rows = pl.ds(b, 32)
                other = y_own[i, me_y, 1 - me_z, rows, :].astype(f32)
                for k in range(2):
                    other = other + y_got[i, k, 1 - me_z, rows, :].astype(f32)
                y_part[i, rows, :] = other.astype(bf16)
                return 0

            blocks(add)
            y2_copy(i).start()

    def last(item):
        i, t = item[1], tile_of(item)
        if item[0] == "z":
            wait_bytes(z_last.at[i], zf_recv.at[i])
        else:
            y2_copy(i).wait_recv()

        def step(b, largest):
            rows = pl.ds(b, 32)
            flat = pl.ds(t * TB + b, 32)
            if item[0] == "z":
                terms = [z_own[me_z, i, me_y, rows, :], z_got[i, me_y, rows, :]]
                terms += [z_last[i, k, rows, :] for k in range(2)]
            else:
                terms = [y_own[i, me_y, me_z, rows, :]] + [y_got[i, k, me_z, rows, :] for k in range(2)]
                terms += [y_last[i, rows, :]]
            grad = functools.reduce(lambda a, b: a + b, [x.astype(f32) for x in terms])
            new = adam(grad, master_v[flat, :], moment_v[flat, :], second_v[flat, :])
            master_out[flat, :], moment_out[flat, :], second_out[flat, :] = new
            return jnp.maximum(largest, jnp.abs(new[0]))

        largest = blocks(step, jnp.zeros((32, TB), f32))
        largest = jnp.max(jnp.max(largest, axis=0, keepdims=True), axis=1, keepdims=True)
        tile_scale = (jnp.broadcast_to(largest, (16, TB)) + scale_epsilon).astype(bf16).astype(f32)
        scale[t] = tile_scale[0:1, :]
        divisor = jnp.broadcast_to(tile_scale[0:1, :], (TB, TB))
        quant[t] = (master_out[t * TB : (t + 1) * TB, :] / divisor).astype(bf16)

    acts = {"r": relay, "m": middle, "l": last}
    steps = (
        "ry0", "mz0", "ry1", "mz1", "ry2", "g0", "mz2", "ry3", "g1", "ry4", "mz3", "tables", "ry5", "rz0", "g2", "my0",
        "ry6", "rz1", "g3", "my1", "mz4", "rz2", "my2", "my3", "rz3", "my4", "states", "lz0", "my5", "lz1", "rz4", "my6",
        "lz2", "ly0", "ly1", "lz3", "ly2", "ly3", "lz4", "ly4", "ly5", "ly6",
    )
    for step in steps:
        if step == "tables":
            index_tables(tab_ref, idx_v, place, me_sh, me_dp)
            idx_copy = pltpu.make_async_copy(idx_v, idx_s, idx_sem)
            idx_copy.start()
        elif step == "states":
            idx_copy.wait()
            for copy in states:
                copy.wait()
        elif step[0] == "g":
            n = int(step[1])
            greeted(n, 2 if n < 3 else 1)
            if n < 3:
                greetings(n + 1, h_next if n < 2 else [core_mate])
        else:
            acts[step[0]]((step[1], int(step[2:])))

    def shard_copy(p, k):
        return remote(stage.at[p, k - 1], arrive[p].at[k - 1], sh_send.at[p], sh_recv.at[p],
                      dict(device_id={"shard": sh_peer(k)}, device_id_type=MESH))

    def scale_copy(k):
        return remote(stage_s.at[k - 1], arrive_s.at[k - 1], ss_send, ss_recv,
                      dict(device_id={"shard": sh_peer(k)}, device_id_type=MESH))

    def to_owners(p):
        rows = slice(p * PR, (p + 1) * PR)

        def stage_step(k, _):
            stage[p, k - 1] = quant[idx_s[k - 1, 0], rows, :]
            if p == 0:
                stage_s[k - 1] = scale[idx_s[k - 1, 0]]
                scale_copy(k).start()
            shard_copy(p, k).start()
            return 0

        lax.fori_loop(1, N_SH, stage_step, 0)
        arrive[p][N_SH - 1] = quant[idx_s[N_SH - 1, 0], rows, :]
        if p == 0:
            arrive_s[N_SH - 1] = scale[idx_s[N_SH - 1, 0]]

    def block_copy(p, d, n, there):
        return remote(whole.at[p, d], whole.at[p, d], ag_send.at[p, n], ag_recv.at[p, n], there)

    def mate_of(k):
        return y_peer(k) * 2 + 1 - me_z

    def same_of(k):
        return y_peer(k) * 2 + me_z

    def own_copies(p):
        return [block_copy(p, me_dp, 0, to_dp(z_mate)), block_copy(p, me_dp, 1, to_y(NEXT)), block_copy(p, me_dp, 2, to_y(PREVIOUS))]

    def mate_copies(p):
        return [block_copy(p, z_mate, 3, to_y(NEXT)), block_copy(p, z_mate, 4, to_y(PREVIOUS))]

    def on_copies(p):
        return [block_copy(p, same_of(PREVIOUS), 5, to_y(NEXT)), block_copy(p, mate_of(NEXT), 6, to_y(PREVIOUS))]

    def gather_scale_copy(k):
        return remote(whole_s.at[me_dp], whole_s.at[me_dp], as_send.at[k], as_recv.at[k], to_dp(dp_peer(k)))

    def pack(p):
        wait_bytes(arrive[p].at[pl.ds(0, N_SH - 1)], sh_recv.at[p])
        for i in range(NT):
            whole[p, me_dp, i] = arrive[p][idx_s[N_SH + i, 0]]
        start(own_copies(p))

    def pass_mate(p):
        own_copies(p)[0].wait_recv()
        start(mate_copies(p))

    def pass_same(p):
        own_copies(p)[1].wait_recv()
        on_copies(p)[0].start()

    def pass_other(p):
        mate_copies(p)[1].wait_recv()
        on_copies(p)[1].start()

    for p in range(AHEAD):
        to_owners(p)
    for p in range(PIECES + 2):
        if p < PIECES:
            pack(p)
        if p + AHEAD < PIECES:
            to_owners(p + AHEAD)
        if p == 0:
            wait_bytes(arrive_s.at[pl.ds(0, N_SH - 1)], ss_recv)
            for i in range(NT):
                whole_s[me_dp, i] = arrive_s[idx_s[N_SH + i, 0]]
            for k in range(1, N_DP):
                gather_scale_copy(k).start()
        if 0 <= p - 1 < PIECES:
            pass_mate(p - 1)
            pass_same(p - 1)
        if 0 <= p - 2 < PIECES:
            pass_other(p - 2)

    for a in range(NZ):
        for copy in [z1_copy(a)] + z_relays(a) + z_owns(a) + z_sums(a):
            copy.wait_send()
    for b in range(NY):
        for copy in [y2_copy(b)] + y_relays(b) + y_owns(b) + y_sums(b):
            copy.wait_send()
    wait_bytes(stage_s.at[pl.ds(0, N_SH - 1)], ss_send)
    for p in range(PIECES):
        wait_bytes(stage.at[p, pl.ds(0, N_SH - 1)], sh_send.at[p])
        own, mate, on = own_copies(p), mate_copies(p), on_copies(p)
        for copy in own + mate + on:
            copy.wait_send()
        for copy in [own[2], mate[0]] + on:
            copy.wait_recv()
    for k in range(1, N_DP):
        gather_scale_copy(k).wait()


def place_kernel(whole, whole_s, place, master_v, moment_v, second_v, tiles, scales, master_out, moment_out, second_out, sem, tile_sem):
    copies = [
        pltpu.make_async_copy(a, b, sem.at[i])
        for i, (a, b) in enumerate(((master_v, master_out), (moment_v, moment_out), (second_v, second_out)))
    ]

    def start(s, _):
        pltpu.make_async_copy(whole.at[:, place[s, 0]], tiles.at[s], tile_sem).start()
        return 0

    lax.fori_loop(0, OWNED, start, 0)
    for copy in copies:
        copy.start()
    lane = lax.broadcasted_iota(jnp.int32, (1, TB), 1)

    def collect(s, acc):
        return jnp.where(lane == s, whole_s[place[s, 0]], acc)

    row = lax.fori_loop(0, OWNED, collect, jnp.zeros((1, TB), jnp.float32))
    scales[...] = row.astype(jnp.bfloat16)[0, :OWNED]
    wait_bytes(tiles, tile_sem)
    for copy in copies:
        copy.wait()


def per_device(gradients, tile_table, master, moment, second):
    shape = master.shape
    flat = (NT * TB, TB)
    f32, bf16 = jnp.float32, jnp.bfloat16
    anywhere = pl.BlockSpec(memory_space=pltpu.HBM)
    vmem = pl.BlockSpec(memory_space=pltpu.VMEM)
    smem = pl.BlockSpec(memory_space=pltpu.SMEM)
    dma = pltpu.SemaphoreType.DMA
    state = jax.ShapeDtypeStruct(flat, f32)
    tile, half = (TB, TB), (HALF, TB)
    outs = pl.pallas_call(
        main_kernel,
        out_shape=(
            pltpu.VMEM(flat, f32), pltpu.VMEM(flat, f32), pltpu.VMEM(flat, f32),
            pltpu.VMEM((PIECES, N_DP, NT, PR, TB), bf16),
            pltpu.VMEM((N_DP, NT, 1, TB), f32),
            pltpu.VMEM((OWNED, TB), jnp.int32),
        ),
        in_specs=[anywhere, vmem, anywhere, anywhere, anywhere],
        out_specs=(vmem,) * 6,
        scratch_shapes=[
            pltpu.VMEM((N_DP, NT * TB * TB), bf16),
            pltpu.VMEM((TB, TB), f32),
            pltpu.VMEM((2, NZ, 4) + tile, bf16),
            pltpu.VMEM((NZ, 4) + tile, bf16),
            pltpu.VMEM((NZ, 3) + tile, bf16),
            pltpu.VMEM((NZ, 2) + half, bf16),
            pltpu.VMEM((NZ, 2) + half, bf16),
            pltpu.VMEM((NZ, 2) + tile, bf16),
            pltpu.VMEM((NY, 4, 2) + tile, bf16),
            pltpu.VMEM((NY, 2, 2) + half, bf16),
            pltpu.VMEM((NY, 2, 2) + half, bf16),
            pltpu.VMEM((NY, 2, 2) + tile, bf16),
            pltpu.VMEM((NY,) + tile, bf16),
            pltpu.VMEM((NY,) + tile, bf16),
            pltpu.VMEM(flat, f32), pltpu.VMEM(flat, f32), pltpu.VMEM(flat, f32),
            pltpu.VMEM((NT,) + tile, bf16),
            pltpu.VMEM((NT, 1, TB), f32),
            pltpu.VMEM((PIECES, N_SH, PR, TB), bf16),
            pltpu.VMEM((N_SH, 1, TB), f32),
            pltpu.VMEM((N_SH, 1, TB), f32),
            pltpu.VMEM((48, TB), jnp.int32),
            pltpu.SMEM((48, TB), jnp.int32),
            *[pltpu.VMEM((N_SH, PR, TB), bf16) for _ in range(PIECES)],
            dma((NT,)), dma((3,)), dma(()),
            dma((NZ,)), dma((NZ,)), dma((NZ,)), dma((NZ, 2)), dma((NZ,)), dma((NZ,)), dma((NZ,)),
            dma((NY,)), dma((NY, 2)), dma((NY,)), dma((NY,)), dma((NY,)), dma((NY,)), dma((NY,)),
            dma((PIECES,)), dma((PIECES,)),
            dma(()), dma(()),
            dma((PIECES, 7)), dma((PIECES, 7)),
            dma((N_DP,)), dma((N_DP,)),
            pltpu.SemaphoreType.REGULAR((4,)),
        ],
        compiler_params=pltpu.CompilerParams(collective_id=0, has_side_effects=True, vmem_limit_bytes=58 << 20),
    )(
        gradients.reshape(N_DP, NT * TB * TB), tile_table,
        master.reshape(flat), moment.reshape(flat), second.reshape(flat),
    )
    master_new, moment_new, second_new, whole, whole_s, place = outs
    tiles, scales, master_new, moment_new, second_new = pl.pallas_call(
        place_kernel,
        out_shape=(
            jax.ShapeDtypeStruct((OWNED, PIECES, PR, TB), bf16),
            jax.ShapeDtypeStruct((OWNED,), bf16),
            state, state, state,
        ),
        in_specs=[vmem, vmem, smem, vmem, vmem, vmem],
        out_specs=(anywhere, vmem, anywhere, anywhere, anywhere),
        scratch_shapes=[dma((3,)), dma(())],
        compiler_params=pltpu.CompilerParams(vmem_limit_bytes=16 << 20),
    )(whole.reshape(PIECES, OWNED, PR, TB), whole_s.reshape(OWNED, 1, TB), place, master_new, moment_new, second_new)
    return (
        master_new.reshape(shape), moment_new.reshape(shape), second_new.reshape(shape),
        tiles.reshape(OWNED, TB, TB), scales,
    )


def solution(mesh):
    in_specs = (
        P("dp", "shard", None, None),
        P(),
        P("shard", "dp", None),
        P("shard", "dp", None),
        P("shard", "dp", None),
    )
    out_specs = (
        P("shard", "dp", None),
        P("shard", "dp", None),
        P("shard", "dp", None),
        P("shard", None, None),
        P("shard"),
    )
    return jax.shard_map(
        per_device, mesh=mesh, in_specs=in_specs, out_specs=out_specs, check_vma=False
    )
```

```python
import functools

import jax
import jax.numpy as jnp
from jax import lax
from jax.experimental import pallas as pl
from jax.experimental.pallas import tpu as pltpu
from jax.sharding import PartitionSpec as P

TB = 128
beta_first = 0.9
beta_second = 0.95
learning_rate = 0.002
weight_decay = 0.1
adam_epsilon = 1e-08
scale_epsilon = 1e-06
step_count = 10

MESH = pl.DeviceIdType.MESH
N_DP = 8
N_SH = 32
NT = 12
OWNED = 96
NZ = 4
NY = NT - NZ
PIECES = 8
PR = TB // PIECES
STEPS = (
    "S0", "S1", "S2", "m0", "g0", "r0", "S3", "m1", "S4", "g1", "s0", "r1", "S5", "n0", "S6", "g2",
    "s1", "r2", "m2", "S7", "x0", "m3", "g3", "r3", "L0", "n1", "T0", "L1", "n2", "s2", "m4", "r4",
    "T1", "r5", "n3", "n4", "m5", "s3", "r6", "r7", "n5", "s4", "L2", "T2", "P0", "L3", "n6", "s5",
    "T3", "P1", "m6", "M0", "L4", "T4", "s6", "L5", "m7", "N0", "M1", "n7", "O0", "T5", "N1", "L6",
    "P2", "T6", "s7", "P3", "N2", "M2", "L7", "T7", "P4", "N3", "O1", "P5", "O2", "N4", "M3", "N5",
    "P6", "M4", "M5", "O3", "N6", "P7", "M6", "O4", "M7", "N7", "O5", "O6", "O7",
)


def wait_bytes(ref, sem):
    pltpu.make_async_copy(ref, ref, sem).wait()


def lane_sum(x):
    return jnp.sum(x, axis=1, keepdims=True)


def index_tables(tab_ref, idx_ref, place_ref, me_sh, me_dp):
    def iota(shape, dim):
        return lax.broadcasted_iota(jnp.int32, shape, dim)

    lane32 = iota((N_SH, OWNED), 1)
    row32 = iota((N_SH, OWNED), 0)
    mine = tab_ref[pl.ds(me_sh, 1), :]
    owner = ((mine >> 5) * 171) >> 9
    offset = jnp.broadcast_to((owner - me_sh - 1) & (N_SH - 1), (N_SH, OWNED))
    col = lane32 - me_dp * NT
    hit = (offset == row32) & (col >= 0) & (col < NT)
    idx_ref[0:N_SH, :] = jnp.broadcast_to(jnp.minimum(lane_sum(jnp.where(hit, col, 0)), NT - 1), (N_SH, TB))

    slot = iota((OWNED, OWNED), 0)
    lane = iota((OWNED, OWNED), 1)
    wanted = slot + me_sh * OWNED

    def find(j, acc):
        row = jnp.broadcast_to(tab_ref[pl.ds(j, 1), :], (OWNED, OWNED))
        return acc + jnp.where(row == wanted, lane + j * TB, 0)

    found = lane_sum(lax.fori_loop(0, N_SH, find, jnp.zeros((OWNED, OWNED), jnp.int32)))
    found = jnp.broadcast_to(found, (OWNED, OWNED))
    source = found >> 7
    part = ((found & (TB - 1)) * 43) >> 9

    def as_row(x):
        return jnp.sum(jnp.where(slot == lane, x, 0), axis=0, keepdims=True)

    part_row = jnp.broadcast_to(as_row(part), (OWNED, OWNED))
    rank = lane_sum(jnp.where((part_row == part) & (lane < slot), 1, 0))
    rank = jnp.broadcast_to(rank, (OWNED, OWNED))
    place_ref[...] = jnp.broadcast_to(jnp.clip(part * NT + rank, 0, OWNED - 1)[:, 0:1], (OWNED, TB))
    arrival = as_row((me_sh - source - 1) & (N_SH - 1))
    key = as_row(jnp.where(part == me_dp, rank, -1))
    row16 = iota((16, OWNED), 0)
    pick = jnp.where(jnp.broadcast_to(key, (16, OWNED)) == row16, jnp.broadcast_to(arrival, (16, OWNED)), 0)
    idx_ref[N_SH : N_SH + 16, :] = jnp.broadcast_to(lane_sum(pick) & (N_SH - 1), (16, TB))


def adam(grad, master, moment, second):
    moment_new = beta_first * moment + (1.0 - beta_first) * grad
    second_new = beta_second * second + (1.0 - beta_second) * grad * grad
    first_fix = 1.0 - beta_first**step_count
    second_fix = 1.0 - beta_second**step_count
    update = moment_new / first_fix / (jnp.sqrt(second_new / second_fix) + adam_epsilon)
    master_new = master - learning_rate * (update + weight_decay * master)
    return master_new, moment_new, second_new


def main_kernel(
    g_hbm, tab_ref, master_hbm, moment_hbm, second_hbm,
    master_out, moment_out, second_out, whole, whole_s, place,
    g_v, spread, z_own, z_got, z_part, z_relay, z_sum, z_last,
    y_own, y_relay, y_sum, y_got, y_part, y_last,
    master_v, moment_v, second_v, largest, scale, stage, stage_s, arrive_s, idx_v, idx_s, *rest,
):
    arrive, narrow = rest[:PIECES], rest[PIECES : 2 * PIECES]
    (
        in_sem, st_sem, idx_sem,
        z1_send, z1_recv, zr_send, zr_recv, zo_send, zs_send, zf_recv,
        yr_send, yr_recv, yo_send, ys_send, yf_recv, y2_send, y2_recv,
        sh_send, sh_recv, ss_send, ss_recv, ag_send, ag_recv, as_send, as_recv, greet,
    ) = rest[2 * PIECES :]
    me_dp = lax.axis_index("dp")
    me_sh = lax.axis_index("shard")
    me_y, me_z = me_dp // 2, me_dp % 2
    me_x, me_h, me_c = me_sh // 8, (me_sh // 2) % 4, me_sh % 2

    def dp_peer(k):
        return lax.rem(me_dp + k, N_DP)

    def sh_peer(k):
        return lax.rem(me_sh + k, N_SH)

    def y_peer(k):
        return lax.rem(me_y + k, 4)

    def to_dp(d):
        return dict(device_id={"dp": d}, device_id_type=MESH)

    def to_y(k):
        return to_dp(y_peer(k) * 2 + me_z)

    z_mate = me_y * 2 + 1 - me_z
    core_mate = {"shard": me_sh + 1 - 2 * me_c}
    x_next = [{"shard": lax.rem(me_x + k, 4) * 8 + me_h * 2 + me_c} for k in (1, 3)]
    h_next = [{"shard": me_x * 8 + lax.rem(me_h + k, 4) * 2 + me_c} for k in (1, 3)]
    f32, bf16 = jnp.float32, jnp.bfloat16
    NEXT, OPPOSITE, PREVIOUS = 1, 2, 3
    ZH, YH = NZ // 2, NY // 2
    Z1, Z2, Y1, Y2 = slice(0, ZH), slice(ZH, NZ), slice(0, YH), slice(YH, NY)
    cols = PR * TB

    barrier = pltpu.get_barrier_semaphore()
    near = [{"dp": z_mate}] + [{"dp": y_peer(k) * 2 + me_z} for k in (1, 2, 3)] + [core_mate] + x_next + h_next
    for device in near:
        pl.semaphore_signal(barrier, 1, device_id=device, device_id_type=MESH)

    def load_gradient(q):
        def one(t, _):
            at = pl.ds(pl.multiple_of(t * TB * TB + q * cols, cols), cols)
            to = pl.ds(pl.multiple_of(t * cols, cols), cols)
            pltpu.make_async_copy(g_hbm.at[:, at], g_v.at[q, :, to], in_sem.at[q]).start()
            return 0

        lax.fori_loop(0, NT, one, 0)

    load_gradient(0)
    states = [
        pltpu.make_async_copy(a, b, st_sem.at[i])
        for i, (a, b) in enumerate(((master_hbm, master_v), (moment_hbm, moment_v), (second_hbm, second_v)))
    ]

    def greetings(stage, devices):
        for device in devices:
            pl.semaphore_signal(greet.at[stage], 1, device_id=device, device_id_type=MESH)

    def remote(src, dst, send, recv, there):
        return pltpu.make_async_remote_copy(src, dst, send, recv, **there)

    def start(*copies):
        for copy in copies:
            copy.start()

    def z1(q):
        return remote(z_own.at[q, 1 - me_z], z_got.at[q], z1_send.at[q], z1_recv.at[q], to_dp(z_mate))

    def zr(q, side):
        part = (Z1, Z2)[side]
        return remote(z_part.at[q, OPPOSITE - 1, part], z_relay.at[q, side], zr_send.at[q], zr_recv.at[q, side],
                      to_y((NEXT, PREVIOUS)[side]))

    def zo(q, side):
        part, k = (Z2, Z1)[side], (NEXT, PREVIOUS)[side]
        return remote(z_part.at[q, k - 1, part], z_last.at[q, side, part], zo_send.at[q], zf_recv.at[q], to_y(k))

    def zs(q, side):
        part, k = (Z1, Z2)[side], (NEXT, PREVIOUS)[side]
        return remote(z_sum.at[q, side], z_last.at[q, side, part], zs_send.at[q], zf_recv.at[q], to_y(k))

    def yr(q, side):
        part = (Y1, Y2)[side]
        return remote(y_own.at[q, y_peer(OPPOSITE), part], y_relay.at[q, side], yr_send.at[q], yr_recv.at[q, side],
                      to_y((NEXT, PREVIOUS)[side]))

    def yo(q, side):
        part, k = (Y2, Y1)[side], (NEXT, PREVIOUS)[side]
        return remote(y_own.at[q, y_peer(k), part], y_got.at[q, side, part], yo_send.at[q], yf_recv.at[q], to_y(k))

    def ys(q, side):
        part, k = (Y1, Y2)[side], (NEXT, PREVIOUS)[side]
        return remote(y_sum.at[q, side], y_got.at[q, side, part], ys_send.at[q], yf_recv.at[q], to_y(k))

    def y2(q):
        return remote(y_part.at[q], y_last.at[q], y2_send.at[q], y2_recv.at[q], to_dp(z_mate))

    def split(q):
        wait_bytes(g_v.at[q], in_sem.at[q])

        def one(t, put):
            for r in range(PR // 16):
                at = pl.multiple_of(t * cols + r * 2048, 2048)
                for u in range(16):
                    spread[u * 8 : u * 8 + 8, :] = g_v[q, :, pl.ds(at + u * TB, TB)].astype(f32)
                for i in range(N_DP):
                    put(i, slice(r * 16, r * 16 + 16), spread[pl.ds(i, 16, stride=8), :].astype(bf16))

        def one_z(a, _):
            def put(i, rows, value):
                z_own[q, i % 2, i // 2, a, rows, :] = value

            one(a, put)
            return 0

        def one_y(b, _):
            def put(i, rows, value):
                y_own[q, i // 2, b, i % 2, rows, :] = value

            one(b + NZ, put)
            return 0

        lax.fori_loop(0, NY, one_y, 0)
        lax.fori_loop(0, NZ, one_z, 0)
        if q == 0:
            pl.semaphore_wait(barrier, len(near))
        start(yr(q, 0), yr(q, 1), yo(q, 0), yo(q, 1), z1(q))
        if q == 0:
            greetings(0, x_next)
            for p in range(1, PIECES):
                load_gradient(p)
            start(*states)

    def wide(x):
        return x.astype(f32)

    def y_relay_step(q):
        yr(q, 0).wait_recv()
        yr(q, 1).wait_recv()

        def add(b, _):
            y_sum[q, 0, b] = (wide(y_own[q, y_peer(NEXT), b]) + wide(y_relay[q, 0, b])).astype(bf16)
            y_sum[q, 1, b] = (wide(y_own[q, y_peer(PREVIOUS), b + YH]) + wide(y_relay[q, 1, b])).astype(bf16)
            return 0

        lax.fori_loop(0, YH, add, 0, unroll=2)
        start(ys(q, 0), ys(q, 1))

    def z_middle(q):
        z1(q).wait_recv()
        for k in (OPPOSITE, NEXT, PREVIOUS):
            y = y_peer(k)
            z_part[q, k - 1] = (wide(z_own[q, me_z, y]) + wide(z_got[q, y])).astype(bf16)
        start(zr(q, 0), zr(q, 1), zo(q, 0), zo(q, 1))

    def z_relay_step(q):
        zr(q, 0).wait_recv()
        zr(q, 1).wait_recv()
        z_sum[q, 0] = (wide(z_part[q, NEXT - 1, Z1]) + wide(z_relay[q, 0])).astype(bf16)
        z_sum[q, 1] = (wide(z_part[q, PREVIOUS - 1, Z2]) + wide(z_relay[q, 1])).astype(bf16)
        start(zs(q, 0), zs(q, 1))

    def y_middle(q):
        wait_bytes(y_got.at[q], yf_recv.at[q])
        for part in (Y1, Y2):
            total = wide(y_own[q, me_y, part, 1 - me_z])
            for side in range(2):
                total = total + wide(y_got[q, side, part, 1 - me_z])
            y_part[q, part] = total.astype(bf16)
        y2(q).start()

    def update(q):
        wait_bytes(z_last.at[q], zf_recv.at[q])
        y2(q).wait_recv()
        if q == 0:
            for copy in states:
                copy.wait()
        rows = slice(q * PR, q * PR + PR)
        groups = [(0, NZ, None)] + [(NZ + part.start, NZ + part.stop, part) for part in (Y1, Y2)]
        for first, stop, part in groups:
            if part is None:
                terms = [z_own[q, me_z, me_y], z_got[q, me_y], z_last[q, 0], z_last[q, 1]]
            else:
                terms = [y_own[q, me_y, part, me_z], y_got[q, 0, part, me_z], y_got[q, 1, part, me_z], y_last[q, part]]
            grad = functools.reduce(lambda a, b: a + b, [wide(x) for x in terms])
            tiles = slice(first, stop)
            new = adam(grad, master_v[tiles, rows, :], moment_v[tiles, rows, :], second_v[tiles, rows, :])
            master_out[tiles, rows, :], moment_out[tiles, rows, :], second_out[tiles, rows, :] = new
            narrow[q][tiles] = new[0].astype(bf16)
            size = jnp.abs(new[0])
            largest[tiles] = size if q == 0 else jnp.maximum(largest[tiles], size)
        if q == PIECES - 1:
            for t in range(NT):
                peak = jnp.max(jnp.max(largest[t], axis=0, keepdims=True), axis=1, keepdims=True)
                rounded = (jnp.broadcast_to(peak, (16, TB)) + scale_epsilon).astype(bf16)
                scale[t] = wide(rounded)[0:1, :]

    def shard_copy(p, k):
        return remote(stage.at[p, k - 1], arrive[p].at[k - 1], sh_send.at[p], sh_recv.at[p],
                      dict(device_id={"shard": sh_peer(k)}, device_id_type=MESH))

    def scale_copy(k):
        return remote(stage_s.at[k - 1], arrive_s.at[k - 1], ss_send, ss_recv,
                      dict(device_id={"shard": sh_peer(k)}, device_id_type=MESH))

    def to_owners(p):
        def stage_step(k, _):
            stage[p, k - 1] = narrow[p][idx_s[k - 1, 0]]
            if p == PIECES - 1:
                stage_s[k - 1] = scale[idx_s[k - 1, 0]]
                scale_copy(k).start()
            shard_copy(p, k).start()
            return 0

        lax.fori_loop(1, N_SH, stage_step, 0)
        arrive[p][N_SH - 1] = narrow[p][idx_s[N_SH - 1, 0]]
        if p == PIECES - 1:
            arrive_s[N_SH - 1] = scale[idx_s[N_SH - 1, 0]]

    def block_copy(p, d, n, there):
        return remote(whole.at[p, d], whole.at[p, d], ag_send.at[p, n], ag_recv.at[p, n], there)

    def gather_copy(p, n):
        k = (None, NEXT, PREVIOUS, NEXT, PREVIOUS, NEXT, PREVIOUS)[n]
        if n == 0:
            return block_copy(p, me_dp, n, to_dp(z_mate))
        block = me_dp if n < 3 else z_mate
        if n == 5:
            block = y_peer(PREVIOUS) * 2 + me_z
        if n == 6:
            block = y_peer(NEXT) * 2 + 1 - me_z
        return block_copy(p, block, n, to_y(k))

    def gather_scale_copy(k):
        return remote(whole_s.at[me_dp], whole_s.at[me_dp], as_send.at[k], as_recv.at[k], to_dp(dp_peer(k)))

    def pack(p):
        if p == PIECES - 1:
            wait_bytes(arrive_s.at[pl.ds(0, N_SH - 1)], ss_recv)
            for i in range(NT):
                whole_s[me_dp, i] = arrive_s[idx_s[N_SH + i, 0]]
            for k in range(1, N_DP):
                gather_scale_copy(k).start()
        wait_bytes(arrive[p].at[pl.ds(0, N_SH - 1)], sh_recv.at[p])
        for i in range(NT):
            whole[p, me_dp, i] = arrive[p][idx_s[N_SH + i, 0]]
        start(gather_copy(p, 0), gather_copy(p, 1), gather_copy(p, 2))

    def pass_mate(p):
        gather_copy(p, 0).wait_recv()
        start(gather_copy(p, 3), gather_copy(p, 4))

    def pass_same(p):
        gather_copy(p, 1).wait_recv()
        gather_copy(p, 5).start()

    def pass_other(p):
        gather_copy(p, 4).wait_recv()
        gather_copy(p, 6).start()

    def tables(_):
        index_tables(tab_ref, idx_v, place, me_sh, me_dp)
        copy = pltpu.make_async_copy(idx_v, idx_s, idx_sem)
        copy.start()
        copy.wait()

    def meet(n):
        pl.semaphore_wait(greet.at[n], 2 if n < 3 else 1)
        if n < 3:
            greetings(n + 1, h_next if n < 2 else [core_mate])

    acts = {
        "S": split, "r": y_relay_step, "m": z_middle, "s": z_relay_step, "n": y_middle, "L": update,
        "T": to_owners, "P": pack, "M": pass_mate, "N": pass_same, "O": pass_other, "x": tables, "g": meet,
    }
    for step in STEPS:
        acts[step[0]](int(step[1:]))

    for q in range(PIECES):
        z1(q).wait_send()
        y2(q).wait_send()
        for side in range(2):
            for copy in (zr, zo, zs, yr, yo, ys):
                copy(q, side).wait_send()
        wait_bytes(stage.at[q, pl.ds(0, N_SH - 1)], sh_send.at[q])
        for n in range(7):
            gather_copy(q, n).wait_send()
        for n in (2, 3, 5, 6):
            gather_copy(q, n).wait_recv()
    wait_bytes(stage_s.at[pl.ds(0, N_SH - 1)], ss_send)
    for k in range(1, N_DP):
        gather_scale_copy(k).wait()


def place_kernel(
    whole, whole_s, place, master_v, moment_v, second_v, tiles, scales, master_out, moment_out, second_out,
    ready, sem, tile_sem,
):
    copies = [
        pltpu.make_async_copy(a, b, sem.at[i])
        for i, (a, b) in enumerate(((master_v, master_out), (moment_v, moment_out), (second_v, second_out)))
    ]
    for copy in copies:
        copy.start()
    lane = lax.broadcasted_iota(jnp.int32, (1, TB), 1)

    def step(s, row):
        at = place[s, 0]
        tile_scale = whole_s[at]
        inverse = jnp.broadcast_to(1.0 / tile_scale, (PR, TB))
        ready[s] = (whole[:, at].astype(jnp.float32) * inverse).astype(jnp.bfloat16)
        pltpu.make_async_copy(ready.at[s], tiles.at[s], tile_sem).start()
        return jnp.where(lane == s, tile_scale, row)

    row = lax.fori_loop(0, OWNED, step, jnp.zeros((1, TB), jnp.float32), unroll=4)
    scales[...] = row.astype(jnp.bfloat16)[0, :OWNED]
    wait_bytes(tiles, tile_sem)
    for copy in copies:
        copy.wait()


def per_device(gradients, tile_table, master, moment, second):
    shape = master.shape
    flat = (NT, TB, TB)
    f32, bf16 = jnp.float32, jnp.bfloat16
    anywhere = pl.BlockSpec(memory_space=pltpu.HBM)
    vmem = pl.BlockSpec(memory_space=pltpu.VMEM)
    smem = pl.BlockSpec(memory_space=pltpu.SMEM)
    dma = pltpu.SemaphoreType.DMA
    state = jax.ShapeDtypeStruct(flat, f32)
    piece = (PR, TB)
    outs = pl.pallas_call(
        main_kernel,
        out_shape=(
            pltpu.VMEM(flat, f32), pltpu.VMEM(flat, f32), pltpu.VMEM(flat, f32),
            pltpu.VMEM((PIECES, N_DP, NT, PR, TB), bf16),
            pltpu.VMEM((N_DP, NT, 1, TB), f32),
            pltpu.VMEM((OWNED, TB), jnp.int32),
        ),
        in_specs=[anywhere, vmem, anywhere, anywhere, anywhere],
        out_specs=(vmem,) * 6,
        scratch_shapes=[
            pltpu.VMEM((PIECES, N_DP, NT * PR * TB), bf16),
            pltpu.VMEM((TB, TB), f32),
            pltpu.VMEM((PIECES, 2, 4, NZ) + piece, bf16),
            pltpu.VMEM((PIECES, 4, NZ) + piece, bf16),
            pltpu.VMEM((PIECES, 3, NZ) + piece, bf16),
            pltpu.VMEM((PIECES, 2, NZ // 2) + piece, bf16),
            pltpu.VMEM((PIECES, 2, NZ // 2) + piece, bf16),
            pltpu.VMEM((PIECES, 2, NZ) + piece, bf16),
            pltpu.VMEM((PIECES, 4, NY, 2) + piece, bf16),
            pltpu.VMEM((PIECES, 2, NY // 2, 2) + piece, bf16),
            pltpu.VMEM((PIECES, 2, NY // 2, 2) + piece, bf16),
            pltpu.VMEM((PIECES, 2, NY, 2) + piece, bf16),
            pltpu.VMEM((PIECES, NY) + piece, bf16),
            pltpu.VMEM((PIECES, NY) + piece, bf16),
            pltpu.VMEM(flat, f32), pltpu.VMEM(flat, f32), pltpu.VMEM(flat, f32),
            pltpu.VMEM((NT,) + piece, f32),
            pltpu.VMEM((NT, 1, TB), f32),
            pltpu.VMEM((PIECES, N_SH) + piece, bf16),
            pltpu.VMEM((N_SH, 1, TB), f32),
            pltpu.VMEM((N_SH, 1, TB), f32),
            pltpu.VMEM((48, TB), jnp.int32),
            pltpu.SMEM((48, TB), jnp.int32),
            *[pltpu.VMEM((N_SH,) + piece, bf16)] * PIECES,
            *[pltpu.VMEM((NT,) + piece, bf16)] * PIECES,
            dma((PIECES,)), dma((3,)), dma(()),
            *[dma((PIECES,))] * 3, dma((PIECES, 2)), *[dma((PIECES,))] * 3,
            dma((PIECES,)), dma((PIECES, 2)), *[dma((PIECES,))] * 5,
            dma((PIECES,)), dma((PIECES,)),
            dma(()), dma(()),
            dma((PIECES, 7)), dma((PIECES, 7)),
            dma((N_DP,)), dma((N_DP,)),
            pltpu.SemaphoreType.REGULAR((4,)),
        ],
        compiler_params=pltpu.CompilerParams(collective_id=0, has_side_effects=True, vmem_limit_bytes=58 << 20),
    )(
        gradients.reshape(N_DP, NT * TB * TB), tile_table,
        master.reshape(flat), moment.reshape(flat), second.reshape(flat),
    )
    master_new, moment_new, second_new, whole, whole_s, place = outs
    tiles, scales, master_new, moment_new, second_new = pl.pallas_call(
        place_kernel,
        out_shape=(
            jax.ShapeDtypeStruct((OWNED, PIECES, PR, TB), bf16),
            jax.ShapeDtypeStruct((OWNED,), bf16),
            state, state, state,
        ),
        in_specs=[vmem, vmem, smem, vmem, vmem, vmem],
        out_specs=(anywhere, vmem, anywhere, anywhere, anywhere),
        scratch_shapes=[pltpu.VMEM((OWNED, PIECES) + piece, bf16), dma((3,)), dma(())],
        compiler_params=pltpu.CompilerParams(vmem_limit_bytes=16 << 20),
    )(whole.reshape(PIECES, OWNED, PR, TB), whole_s.reshape(OWNED, 1, TB), place, master_new, moment_new, second_new)
    return (
        master_new.reshape(shape), moment_new.reshape(shape), second_new.reshape(shape),
        tiles.reshape(OWNED, TB, TB), scales,
    )


def solution(mesh):
    in_specs = (
        P("dp", "shard", None, None),
        P(),
        P("shard", "dp", None),
        P("shard", "dp", None),
        P("shard", "dp", None),
    )
    out_specs = (
        P("shard", "dp", None),
        P("shard", "dp", None),
        P("shard", "dp", None),
        P("shard", None, None),
        P("shard"),
    )
    return jax.shard_map(
        per_device, mesh=mesh, in_specs=in_specs, out_specs=out_specs, check_vma=False
    )
```

```python
import functools

import jax
import jax.numpy as jnp
from jax import lax
from jax.experimental import pallas as pl
from jax.experimental.pallas import tpu as pltpu
from jax.sharding import PartitionSpec as P

TB = 128
beta_first = 0.9
beta_second = 0.95
learning_rate = 0.002
weight_decay = 0.1
adam_epsilon = 1e-08
scale_epsilon = 1e-06
step_count = 10

MESH = pl.DeviceIdType.MESH
N_DP = 8
N_SH = 32
NT = 12
OWNED = 96
NZ = 4
NY = NT - NZ
PIECES = 8
PR = TB // PIECES
STEPS = (
    "S0", "S1", "S2", "m0", "g0", "r0", "S3", "m1", "S4", "g1", "r1", "s0", "S5", "n0", "S6", "g2",
    "r2", "s1", "m2", "m3", "r3", "S7", "x0", "g3", "n1", "L0", "T0", "r4", "n2", "L1", "T1", "n3",
    "s2", "r5", "m4", "m5", "s3", "n4", "L2", "n5", "T2", "r6", "s4", "m6", "m7", "L3", "s5", "r7",
    "n6", "P0", "T3", "P1", "L4", "T4", "s6", "n7", "P2", "L5", "s7", "N0", "L6", "T5", "M0", "P3",
    "L7", "O0", "T6", "N1", "M1", "N2", "M2", "N3", "T7", "P4", "M3", "O1", "P5", "N4", "O2", "O3",
    "N5", "M4", "P6", "M5", "P7", "O4", "M6", "M7", "N6", "O5", "O6", "N7", "O7",
)


def wait_bytes(ref, sem):
    pltpu.make_async_copy(ref, ref, sem).wait()


def lane_sum(x):
    return jnp.sum(x, axis=1, keepdims=True)


def index_tables(tab_ref, idx_ref, place_ref, me_sh, me_dp):
    def iota(shape, dim):
        return lax.broadcasted_iota(jnp.int32, shape, dim)

    lane32 = iota((N_SH, OWNED), 1)
    row32 = iota((N_SH, OWNED), 0)
    mine = tab_ref[pl.ds(me_sh, 1), :]
    owner = ((mine >> 5) * 171) >> 9
    offset = jnp.broadcast_to((owner - me_sh - 1) & (N_SH - 1), (N_SH, OWNED))
    col = lane32 - me_dp * NT
    hit = (offset == row32) & (col >= 0) & (col < NT)
    idx_ref[0:N_SH, :] = jnp.broadcast_to(jnp.minimum(lane_sum(jnp.where(hit, col, 0)), NT - 1), (N_SH, TB))

    slot = iota((OWNED, OWNED), 0)
    lane = iota((OWNED, OWNED), 1)
    wanted = slot + me_sh * OWNED

    def find(j, acc):
        row = jnp.broadcast_to(tab_ref[pl.ds(j, 1), :], (OWNED, OWNED))
        return acc + jnp.where(row == wanted, lane + j * TB, 0)

    found = lane_sum(lax.fori_loop(0, N_SH, find, jnp.zeros((OWNED, OWNED), jnp.int32)))
    found = jnp.broadcast_to(found, (OWNED, OWNED))
    source = found >> 7
    part = ((found & (TB - 1)) * 43) >> 9

    def as_row(x):
        return jnp.sum(jnp.where(slot == lane, x, 0), axis=0, keepdims=True)

    part_row = jnp.broadcast_to(as_row(part), (OWNED, OWNED))
    rank = lane_sum(jnp.where((part_row == part) & (lane < slot), 1, 0))
    rank = jnp.broadcast_to(rank, (OWNED, OWNED))
    place_ref[...] = jnp.broadcast_to(jnp.clip(part * NT + rank, 0, OWNED - 1)[:, 0:1], (OWNED, TB))
    arrival = as_row((me_sh - source - 1) & (N_SH - 1))
    key = as_row(jnp.where(part == me_dp, rank, -1))
    row16 = iota((16, OWNED), 0)
    pick = jnp.where(jnp.broadcast_to(key, (16, OWNED)) == row16, jnp.broadcast_to(arrival, (16, OWNED)), 0)
    idx_ref[N_SH : N_SH + 16, :] = jnp.broadcast_to(lane_sum(pick) & (N_SH - 1), (16, TB))


def adam(grad, master, moment, second):
    moment_new = beta_first * moment + (1.0 - beta_first) * grad
    second_new = beta_second * second + (1.0 - beta_second) * grad * grad
    first_fix = 1.0 - beta_first**step_count
    second_fix = 1.0 - beta_second**step_count
    update = moment_new / first_fix / (jnp.sqrt(second_new / second_fix) + adam_epsilon)
    master_new = master - learning_rate * (update + weight_decay * master)
    return master_new, moment_new, second_new


def main_kernel(
    g_hbm, tab_ref, master_hbm, moment_hbm, second_hbm,
    master_out, moment_out, second_out, whole, whole_s, place,
    g_v, spread, z_own, z_got, z_part, z_relay, z_sum, z_last,
    y_own, y_relay, y_sum, y_got, y_part, y_last,
    master_v, moment_v, second_v, largest, scale, stage, stage_s, arrive_s, idx_v, idx_s, *rest,
):
    arrive, narrow = rest[:PIECES], rest[PIECES : 2 * PIECES]
    (
        in_sem, st_sem, idx_sem,
        z1_send, z1_recv, zr_send, zr_recv, zo_send, zs_send, zf_recv,
        yr_send, yr_recv, yo_send, ys_send, yf_recv, y2_send, y2_recv,
        sh_send, sh_recv, ss_send, ss_recv, ag_send, ag_recv, as_send, as_recv, greet,
    ) = rest[2 * PIECES :]
    me_dp = lax.axis_index("dp")
    me_sh = lax.axis_index("shard")
    me_y, me_z = me_dp // 2, me_dp % 2
    me_x, me_h, me_c = me_sh // 8, (me_sh // 2) % 4, me_sh % 2

    def dp_peer(k):
        return lax.rem(me_dp + k, N_DP)

    def sh_peer(k):
        return lax.rem(me_sh + k, N_SH)

    def y_peer(k):
        return lax.rem(me_y + k, 4)

    def to_dp(d):
        return dict(device_id={"dp": d}, device_id_type=MESH)

    def to_y(k):
        return to_dp(y_peer(k) * 2 + me_z)

    z_mate = me_y * 2 + 1 - me_z
    core_mate = {"shard": me_sh + 1 - 2 * me_c}
    x_next = [{"shard": lax.rem(me_x + k, 4) * 8 + me_h * 2 + me_c} for k in (1, 3)]
    h_next = [{"shard": me_x * 8 + lax.rem(me_h + k, 4) * 2 + me_c} for k in (1, 3)]
    f32, bf16 = jnp.float32, jnp.bfloat16
    NEXT, OPPOSITE, PREVIOUS = 1, 2, 3
    ZH, YH = NZ // 2, NY // 2
    Z1, Z2, Y1, Y2 = slice(0, ZH), slice(ZH, NZ), slice(0, YH), slice(YH, NY)
    cols = PR * TB

    barrier = pltpu.get_barrier_semaphore()
    near = [{"dp": z_mate}] + [{"dp": y_peer(k) * 2 + me_z} for k in (1, 2, 3)] + [core_mate] + x_next + h_next
    for device in near:
        pl.semaphore_signal(barrier, 1, device_id=device, device_id_type=MESH)

    def load_gradient(q):
        def one(t, _):
            at = pl.ds(pl.multiple_of(t * TB * TB + q * cols, cols), cols)
            to = pl.ds(pl.multiple_of(t * cols, cols), cols)
            pltpu.make_async_copy(g_hbm.at[:, at], g_v.at[q, :, to], in_sem.at[q]).start()
            return 0

        lax.fori_loop(0, NT, one, 0)

    load_gradient(0)
    states = [
        pltpu.make_async_copy(a, b, st_sem.at[i])
        for i, (a, b) in enumerate(((master_hbm, master_v), (moment_hbm, moment_v), (second_hbm, second_v)))
    ]

    def greetings(stage, devices):
        for device in devices:
            pl.semaphore_signal(greet.at[stage], 1, device_id=device, device_id_type=MESH)

    def remote(src, dst, send, recv, there):
        return pltpu.make_async_remote_copy(src, dst, send, recv, **there)

    def start(*copies):
        for copy in copies:
            copy.start()

    def z1(q):
        return remote(z_own.at[q, 1 - me_z], z_got.at[q], z1_send.at[q], z1_recv.at[q], to_dp(z_mate))

    def zr(q, side):
        part = (Z1, Z2)[side]
        return remote(z_part.at[q, OPPOSITE - 1, part], z_relay.at[q, side], zr_send.at[q], zr_recv.at[q, side],
                      to_y((NEXT, PREVIOUS)[side]))

    def zo(q, side):
        part, k = (Z2, Z1)[side], (NEXT, PREVIOUS)[side]
        return remote(z_part.at[q, k - 1, part], z_last.at[q, side, part], zo_send.at[q], zf_recv.at[q], to_y(k))

    def zs(q, side):
        part, k = (Z1, Z2)[side], (NEXT, PREVIOUS)[side]
        return remote(z_sum.at[q, side], z_last.at[q, side, part], zs_send.at[q], zf_recv.at[q], to_y(k))

    def yr(q, side):
        part = (Y1, Y2)[side]
        return remote(y_own.at[q, y_peer(OPPOSITE), part], y_relay.at[q, side], yr_send.at[q], yr_recv.at[q, side],
                      to_y((NEXT, PREVIOUS)[side]))

    def yo(q, side):
        part, k = (Y2, Y1)[side], (NEXT, PREVIOUS)[side]
        return remote(y_own.at[q, y_peer(k), part], y_got.at[q, side, part], yo_send.at[q], yf_recv.at[q], to_y(k))

    def ys(q, side):
        part, k = (Y1, Y2)[side], (NEXT, PREVIOUS)[side]
        return remote(y_sum.at[q, side], y_got.at[q, side, part], ys_send.at[q], yf_recv.at[q], to_y(k))

    def y2(q):
        return remote(y_part.at[q], y_last.at[q], y2_send.at[q], y2_recv.at[q], to_dp(z_mate))

    def split(q):
        wait_bytes(g_v.at[q], in_sem.at[q])

        def one(t, put):
            for r in range(PR // 16):
                at = pl.multiple_of(t * cols + r * 2048, 2048)
                for u in range(16):
                    spread[u * 8 : u * 8 + 8, :] = g_v[q, :, pl.ds(at + u * TB, TB)].astype(f32)
                for i in range(N_DP):
                    put(i, slice(r * 16, r * 16 + 16), spread[pl.ds(i, 16, stride=8), :].astype(bf16))

        def one_z(a, _):
            def put(i, rows, value):
                z_own[q, i % 2, i // 2, a, rows, :] = value

            one(a, put)
            return 0

        def one_y(b, _):
            def put(i, rows, value):
                y_own[q, i // 2, b, i % 2, rows, :] = value

            one(b + NZ, put)
            return 0

        lax.fori_loop(0, NY, one_y, 0)
        lax.fori_loop(0, NZ, one_z, 0)
        if q == 0:
            pl.semaphore_wait(barrier, len(near))
        start(yr(q, 0), yr(q, 1), yo(q, 0), yo(q, 1), z1(q))
        if q == 0:
            greetings(0, x_next)
            for p in range(1, PIECES):
                load_gradient(p)
            start(*states)

    def wide(x):
        return x.astype(f32)

    def y_relay_step(q):
        yr(q, 0).wait_recv()
        yr(q, 1).wait_recv()

        def add(b, _):
            y_sum[q, 0, b] = (wide(y_own[q, y_peer(NEXT), b]) + wide(y_relay[q, 0, b])).astype(bf16)
            y_sum[q, 1, b] = (wide(y_own[q, y_peer(PREVIOUS), b + YH]) + wide(y_relay[q, 1, b])).astype(bf16)
            return 0

        lax.fori_loop(0, YH, add, 0, unroll=2)
        start(ys(q, 0), ys(q, 1))

    def z_middle(q):
        z1(q).wait_recv()
        for k in (OPPOSITE, NEXT, PREVIOUS):
            y = y_peer(k)
            z_part[q, k - 1] = (wide(z_own[q, me_z, y]) + wide(z_got[q, y])).astype(bf16)
        start(zr(q, 0), zr(q, 1), zo(q, 0), zo(q, 1))

    def z_relay_step(q):
        zr(q, 0).wait_recv()
        zr(q, 1).wait_recv()
        z_sum[q, 0] = (wide(z_part[q, NEXT - 1, Z1]) + wide(z_relay[q, 0])).astype(bf16)
        z_sum[q, 1] = (wide(z_part[q, PREVIOUS - 1, Z2]) + wide(z_relay[q, 1])).astype(bf16)
        start(zs(q, 0), zs(q, 1))

    def y_middle(q):
        wait_bytes(y_got.at[q], yf_recv.at[q])
        for part in (Y1, Y2):
            total = wide(y_own[q, me_y, part, 1 - me_z])
            for side in range(2):
                total = total + wide(y_got[q, side, part, 1 - me_z])
            y_part[q, part] = total.astype(bf16)
        y2(q).start()

    def update(q):
        wait_bytes(z_last.at[q], zf_recv.at[q])
        y2(q).wait_recv()
        if q == 0:
            for copy in states:
                copy.wait()
        rows = slice(q * PR, q * PR + PR)
        groups = [(0, NZ, None)] + [(NZ + part.start, NZ + part.stop, part) for part in (Y1, Y2)]
        for first, stop, part in groups:
            if part is None:
                terms = [z_own[q, me_z, me_y], z_got[q, me_y], z_last[q, 0], z_last[q, 1]]
            else:
                terms = [y_own[q, me_y, part, me_z], y_got[q, 0, part, me_z], y_got[q, 1, part, me_z], y_last[q, part]]
            grad = functools.reduce(lambda a, b: a + b, [wide(x) for x in terms])
            tiles = slice(first, stop)
            new = adam(grad, master_v[tiles, rows, :], moment_v[tiles, rows, :], second_v[tiles, rows, :])
            master_out[tiles, rows, :], moment_out[tiles, rows, :], second_out[tiles, rows, :] = new
            narrow[q][tiles] = new[0].astype(bf16)
            size = jnp.abs(new[0])
            largest[tiles] = size if q == 0 else jnp.maximum(largest[tiles], size)
        if q == PIECES - 1:
            for t in range(NT):
                peak = jnp.max(jnp.max(largest[t], axis=0, keepdims=True), axis=1, keepdims=True)
                rounded = (jnp.broadcast_to(peak, (16, TB)) + scale_epsilon).astype(bf16)
                scale[t] = wide(rounded)[0:1, :]

    def shard_copy(p, k):
        return remote(stage.at[p, k - 1], arrive[p].at[k - 1], sh_send.at[p], sh_recv.at[p],
                      dict(device_id={"shard": sh_peer(k)}, device_id_type=MESH))

    def scale_copy(k):
        return remote(stage_s.at[k - 1], arrive_s.at[k - 1], ss_send, ss_recv,
                      dict(device_id={"shard": sh_peer(k)}, device_id_type=MESH))

    def to_owners(p):
        def stage_step(k, _):
            stage[p, k - 1] = narrow[p][idx_s[k - 1, 0]]
            if p == PIECES - 1:
                stage_s[k - 1] = scale[idx_s[k - 1, 0]]
                scale_copy(k).start()
            shard_copy(p, k).start()
            return 0

        lax.fori_loop(1, N_SH, stage_step, 0)
        arrive[p][N_SH - 1] = narrow[p][idx_s[N_SH - 1, 0]]
        if p == PIECES - 1:
            arrive_s[N_SH - 1] = scale[idx_s[N_SH - 1, 0]]

    def block_copy(p, d, n, there):
        return remote(whole.at[p, d], whole.at[p, d], ag_send.at[p, n], ag_recv.at[p, n], there)

    def gather_copy(p, n):
        k = (None, NEXT, PREVIOUS, NEXT, PREVIOUS, NEXT, PREVIOUS)[n]
        if n == 0:
            return block_copy(p, me_dp, n, to_dp(z_mate))
        block = me_dp if n < 3 else z_mate
        if n == 5:
            block = y_peer(PREVIOUS) * 2 + me_z
        if n == 6:
            block = y_peer(NEXT) * 2 + 1 - me_z
        return block_copy(p, block, n, to_y(k))

    def gather_scale_copy(k):
        return remote(whole_s.at[me_dp], whole_s.at[me_dp], as_send.at[k], as_recv.at[k], to_dp(dp_peer(k)))

    def pack(p):
        if p == PIECES - 1:
            wait_bytes(arrive_s.at[pl.ds(0, N_SH - 1)], ss_recv)
            for i in range(NT):
                whole_s[me_dp, i] = arrive_s[idx_s[N_SH + i, 0]]
            for k in range(1, N_DP):
                gather_scale_copy(k).start()
        wait_bytes(arrive[p].at[pl.ds(0, N_SH - 1)], sh_recv.at[p])
        for i in range(NT):
            whole[p, me_dp, i] = arrive[p][idx_s[N_SH + i, 0]]
        start(gather_copy(p, 0), gather_copy(p, 1), gather_copy(p, 2))

    def pass_mate(p):
        gather_copy(p, 0).wait_recv()
        start(gather_copy(p, 3), gather_copy(p, 4))

    def pass_same(p):
        gather_copy(p, 1).wait_recv()
        gather_copy(p, 5).start()

    def pass_other(p):
        gather_copy(p, 4).wait_recv()
        gather_copy(p, 6).start()

    def tables(_):
        index_tables(tab_ref, idx_v, place, me_sh, me_dp)
        copy = pltpu.make_async_copy(idx_v, idx_s, idx_sem)
        copy.start()
        copy.wait()

    def meet(n):
        pl.semaphore_wait(greet.at[n], 2 if n < 3 else 1)
        if n < 3:
            greetings(n + 1, h_next if n < 2 else [core_mate])

    acts = {
        "S": split, "r": y_relay_step, "m": z_middle, "s": z_relay_step, "n": y_middle, "L": update,
        "T": to_owners, "P": pack, "M": pass_mate, "N": pass_same, "O": pass_other, "x": tables, "g": meet,
    }
    for step in STEPS:
        acts[step[0]](int(step[1:]))

    for q in range(PIECES):
        z1(q).wait_send()
        y2(q).wait_send()
        for side in range(2):
            for copy in (zr, zo, zs, yr, yo, ys):
                copy(q, side).wait_send()
        wait_bytes(stage.at[q, pl.ds(0, N_SH - 1)], sh_send.at[q])
        for n in range(7):
            gather_copy(q, n).wait_send()
        for n in (2, 3, 5, 6):
            gather_copy(q, n).wait_recv()
    wait_bytes(stage_s.at[pl.ds(0, N_SH - 1)], ss_send)
    for k in range(1, N_DP):
        gather_scale_copy(k).wait()


def place_kernel(
    whole, whole_s, place, master_v, moment_v, second_v, tiles, scales, master_out, moment_out, second_out,
    ready, sem, tile_sem,
):
    copies = [
        pltpu.make_async_copy(a, b, sem.at[i])
        for i, (a, b) in enumerate(((master_v, master_out), (moment_v, moment_out), (second_v, second_out)))
    ]
    for copy in copies:
        copy.start()
    lane = lax.broadcasted_iota(jnp.int32, (1, TB), 1)

    def step(s, row):
        at = place[s, 0]
        tile_scale = whole_s[at]
        inverse = jnp.broadcast_to(1.0 / tile_scale, (PR, TB))
        ready[s] = (whole[:, at].astype(jnp.float32) * inverse).astype(jnp.bfloat16)
        pltpu.make_async_copy(ready.at[s], tiles.at[s], tile_sem).start()
        return jnp.where(lane == s, tile_scale, row)

    row = lax.fori_loop(0, OWNED, step, jnp.zeros((1, TB), jnp.float32), unroll=4)
    scales[...] = row.astype(jnp.bfloat16)[0, :OWNED]
    wait_bytes(tiles, tile_sem)
    for copy in copies:
        copy.wait()


def per_device(gradients, tile_table, master, moment, second):
    shape = master.shape
    flat = (NT, TB, TB)
    f32, bf16 = jnp.float32, jnp.bfloat16
    anywhere = pl.BlockSpec(memory_space=pltpu.HBM)
    vmem = pl.BlockSpec(memory_space=pltpu.VMEM)
    smem = pl.BlockSpec(memory_space=pltpu.SMEM)
    dma = pltpu.SemaphoreType.DMA
    state = jax.ShapeDtypeStruct(flat, f32)
    piece = (PR, TB)
    outs = pl.pallas_call(
        main_kernel,
        out_shape=(
            pltpu.VMEM(flat, f32), pltpu.VMEM(flat, f32), pltpu.VMEM(flat, f32),
            pltpu.VMEM((PIECES, N_DP, NT, PR, TB), bf16),
            pltpu.VMEM((N_DP, NT, 1, TB), f32),
            pltpu.VMEM((OWNED, TB), jnp.int32),
        ),
        in_specs=[anywhere, vmem, anywhere, anywhere, anywhere],
        out_specs=(vmem,) * 6,
        scratch_shapes=[
            pltpu.VMEM((PIECES, N_DP, NT * PR * TB), bf16),
            pltpu.VMEM((TB, TB), f32),
            pltpu.VMEM((PIECES, 2, 4, NZ) + piece, bf16),
            pltpu.VMEM((PIECES, 4, NZ) + piece, bf16),
            pltpu.VMEM((PIECES, 3, NZ) + piece, bf16),
            pltpu.VMEM((PIECES, 2, NZ // 2) + piece, bf16),
            pltpu.VMEM((PIECES, 2, NZ // 2) + piece, bf16),
            pltpu.VMEM((PIECES, 2, NZ) + piece, bf16),
            pltpu.VMEM((PIECES, 4, NY, 2) + piece, bf16),
            pltpu.VMEM((PIECES, 2, NY // 2, 2) + piece, bf16),
            pltpu.VMEM((PIECES, 2, NY // 2, 2) + piece, bf16),
            pltpu.VMEM((PIECES, 2, NY, 2) + piece, bf16),
            pltpu.VMEM((PIECES, NY) + piece, bf16),
            pltpu.VMEM((PIECES, NY) + piece, bf16),
            pltpu.VMEM(flat, f32), pltpu.VMEM(flat, f32), pltpu.VMEM(flat, f32),
            pltpu.VMEM((NT,) + piece, f32),
            pltpu.VMEM((NT, 1, TB), f32),
            pltpu.VMEM((PIECES, N_SH) + piece, bf16),
            pltpu.VMEM((N_SH, 1, TB), f32),
            pltpu.VMEM((N_SH, 1, TB), f32),
            pltpu.VMEM((48, TB), jnp.int32),
            pltpu.SMEM((48, TB), jnp.int32),
            *[pltpu.VMEM((N_SH,) + piece, bf16)] * PIECES,
            *[pltpu.VMEM((NT,) + piece, bf16)] * PIECES,
            dma((PIECES,)), dma((3,)), dma(()),
            *[dma((PIECES,))] * 3, dma((PIECES, 2)), *[dma((PIECES,))] * 3,
            dma((PIECES,)), dma((PIECES, 2)), *[dma((PIECES,))] * 5,
            dma((PIECES,)), dma((PIECES,)),
            dma(()), dma(()),
            dma((PIECES, 7)), dma((PIECES, 7)),
            dma((N_DP,)), dma((N_DP,)),
            pltpu.SemaphoreType.REGULAR((4,)),
        ],
        compiler_params=pltpu.CompilerParams(collective_id=0, has_side_effects=True, vmem_limit_bytes=58 << 20),
    )(
        gradients.reshape(N_DP, NT * TB * TB), tile_table,
        master.reshape(flat), moment.reshape(flat), second.reshape(flat),
    )
    master_new, moment_new, second_new, whole, whole_s, place = outs
    tiles, scales, master_new, moment_new, second_new = pl.pallas_call(
        place_kernel,
        out_shape=(
            jax.ShapeDtypeStruct((OWNED, PIECES, PR, TB), bf16),
            jax.ShapeDtypeStruct((OWNED,), bf16),
            state, state, state,
        ),
        in_specs=[vmem, vmem, smem, vmem, vmem, vmem],
        out_specs=(anywhere, vmem, anywhere, anywhere, anywhere),
        scratch_shapes=[pltpu.VMEM((OWNED, PIECES) + piece, bf16), dma((3,)), dma(())],
        compiler_params=pltpu.CompilerParams(vmem_limit_bytes=16 << 20),
    )(whole.reshape(PIECES, OWNED, PR, TB), whole_s.reshape(OWNED, 1, TB), place, master_new, moment_new, second_new)
    return (
        master_new.reshape(shape), moment_new.reshape(shape), second_new.reshape(shape),
        tiles.reshape(OWNED, TB, TB), scales,
    )


def solution(mesh):
    in_specs = (
        P("dp", "shard", None, None),
        P(),
        P("shard", "dp", None),
        P("shard", "dp", None),
        P("shard", "dp", None),
    )
    out_specs = (
        P("shard", "dp", None),
        P("shard", "dp", None),
        P("shard", "dp", None),
        P("shard", None, None),
        P("shard"),
    )
    return jax.shard_map(
        per_device, mesh=mesh, in_specs=in_specs, out_specs=out_specs, check_vma=False
    )
```

```python
import functools

import jax
import jax.numpy as jnp
from jax import lax
from jax.experimental import pallas as pl
from jax.experimental.pallas import tpu as pltpu
from jax.sharding import PartitionSpec as P

TB = 128
beta_first = 0.9
beta_second = 0.95
learning_rate = 0.002
weight_decay = 0.1
adam_epsilon = 1e-08
scale_epsilon = 1e-06
step_count = 10

MESH = pl.DeviceIdType.MESH
N_DP = 8
N_SH = 32
NT = 12
OWNED = 96
NZ = 4
NY = NT - NZ
PIECES = 8
PR = TB // PIECES
STEPS = (
    "S0", "S1", "S2", "m0", "g0", "r0", "S3", "m1", "S4", "g1", "r1", "s0", "S5", "n0", "S6", "g2",
    "r2", "s1", "m2", "m3", "r3", "S7", "x0", "g3", "n1", "L0", "T0", "r4", "n2", "L1", "T1", "n3",
    "s2", "r5", "m4", "m5", "s3", "n4", "L2", "n5", "T2", "r6", "s4", "m6", "m7", "L3", "s5", "r7",
    "n6", "P0", "T3", "P1", "L4", "T4", "s6", "n7", "P2", "L5", "s7", "N0", "L6", "T5", "M0", "P3",
    "L7", "O0", "T6", "N1", "M1", "N2", "M2", "N3", "T7", "P4", "M3", "O1", "P5", "N4", "O2", "O3",
    "N5", "M4", "P6", "M5", "P7", "O4", "M6", "M7", "N6", "O5", "O6", "N7", "O7",
)


def wait_bytes(ref, sem):
    pltpu.make_async_copy(ref, ref, sem).wait()


def lane_sum(x):
    return jnp.sum(x, axis=1, keepdims=True)


def index_tables(tab_ref, idx_ref, place_ref, me_sh, me_dp):
    def iota(shape, dim):
        return lax.broadcasted_iota(jnp.int32, shape, dim)

    lane32 = iota((N_SH, OWNED), 1)
    row32 = iota((N_SH, OWNED), 0)
    mine = tab_ref[pl.ds(me_sh, 1), :]
    owner = ((mine >> 5) * 171) >> 9
    offset = jnp.broadcast_to((owner - me_sh - 1) & (N_SH - 1), (N_SH, OWNED))
    col = lane32 - me_dp * NT
    hit = (offset == row32) & (col >= 0) & (col < NT)
    idx_ref[0:N_SH, :] = jnp.broadcast_to(jnp.minimum(lane_sum(jnp.where(hit, col, 0)), NT - 1), (N_SH, TB))

    slot = iota((OWNED, OWNED), 0)
    lane = iota((OWNED, OWNED), 1)
    wanted = slot + me_sh * OWNED

    def find(j, acc):
        row = jnp.broadcast_to(tab_ref[pl.ds(j, 1), :], (OWNED, OWNED))
        return acc + jnp.where(row == wanted, lane + j * TB, 0)

    found = lane_sum(lax.fori_loop(0, N_SH, find, jnp.zeros((OWNED, OWNED), jnp.int32)))
    found = jnp.broadcast_to(found, (OWNED, OWNED))
    source = found >> 7
    part = ((found & (TB - 1)) * 43) >> 9

    def as_row(x):
        return jnp.sum(jnp.where(slot == lane, x, 0), axis=0, keepdims=True)

    part_row = jnp.broadcast_to(as_row(part), (OWNED, OWNED))
    rank = lane_sum(jnp.where((part_row == part) & (lane < slot), 1, 0))
    rank = jnp.broadcast_to(rank, (OWNED, OWNED))
    place_ref[...] = jnp.broadcast_to(jnp.clip(part * NT + rank, 0, OWNED - 1)[:, 0:1], (OWNED, TB))
    arrival = as_row((me_sh - source - 1) & (N_SH - 1))
    key = as_row(jnp.where(part == me_dp, rank, -1))
    row16 = iota((16, OWNED), 0)
    pick = jnp.where(jnp.broadcast_to(key, (16, OWNED)) == row16, jnp.broadcast_to(arrival, (16, OWNED)), 0)
    idx_ref[N_SH : N_SH + 16, :] = jnp.broadcast_to(lane_sum(pick) & (N_SH - 1), (16, TB))


def adam(grad, master, moment, second):
    moment_new = beta_first * moment + (1.0 - beta_first) * grad
    second_new = beta_second * second + (1.0 - beta_second) * grad * grad
    first_fix = 1.0 - beta_first**step_count
    second_fix = 1.0 - beta_second**step_count
    update = moment_new / first_fix / (jnp.sqrt(second_new / second_fix) + adam_epsilon)
    master_new = master - learning_rate * (update + weight_decay * master)
    return master_new, moment_new, second_new


def main_kernel(
    g_hbm, tab_ref, master_hbm, moment_hbm, second_hbm,
    master_out, moment_out, second_out, whole, whole_s, place,
    g_v, spread, z_own, z_got, z_part, z_relay, z_sum, z_last,
    y_own, y_relay, y_sum, y_got, y_part, y_last,
    master_v, moment_v, second_v, largest, scale, stage, stage_s, arrive_s, idx_v, idx_s, *rest,
):
    arrive, narrow = rest[:PIECES], rest[PIECES : 2 * PIECES]
    (
        in_sem, st_sem, idx_sem,
        z1_send, z1_recv, zr_send, zr_recv, zo_send, zs_send, zf_recv,
        yr_send, yr_recv, yo_send, ys_send, yf_recv, y2_send, y2_recv,
        sh_send, sh_recv, ss_send, ss_recv, ag_send, ag_recv, as_send, as_recv, greet,
    ) = rest[2 * PIECES :]
    me_dp = lax.axis_index("dp")
    me_sh = lax.axis_index("shard")
    me_y, me_z = me_dp // 2, me_dp % 2
    me_x, me_h, me_c = me_sh // 8, (me_sh // 2) % 4, me_sh % 2

    def dp_peer(k):
        return lax.rem(me_dp + k, N_DP)

    def sh_peer(k):
        return lax.rem(me_sh + k, N_SH)

    def y_peer(k):
        return lax.rem(me_y + k, 4)

    def to_dp(d):
        return dict(device_id={"dp": d}, device_id_type=MESH)

    def to_y(k):
        return to_dp(y_peer(k) * 2 + me_z)

    z_mate = me_y * 2 + 1 - me_z
    core_mate = {"shard": me_sh + 1 - 2 * me_c}
    x_next = [{"shard": lax.rem(me_x + k, 4) * 8 + me_h * 2 + me_c} for k in (1, 3)]
    h_next = [{"shard": me_x * 8 + lax.rem(me_h + k, 4) * 2 + me_c} for k in (1, 3)]
    f32, bf16 = jnp.float32, jnp.bfloat16
    NEXT, OPPOSITE, PREVIOUS = 1, 2, 3
    ZH, YH = NZ // 2, NY // 2
    Z1, Z2, Y1, Y2 = slice(0, ZH), slice(ZH, NZ), slice(0, YH), slice(YH, NY)
    cols = PR * TB

    barrier = pltpu.get_barrier_semaphore()
    near = [{"dp": z_mate}] + [{"dp": y_peer(k) * 2 + me_z} for k in (1, 2, 3)] + [core_mate] + x_next + h_next
    for device in near:
        pl.semaphore_signal(barrier, 1, device_id=device, device_id_type=MESH)

    def load_gradient(q):
        def one(t, _):
            at = pl.ds(pl.multiple_of(t * TB * TB + q * cols, cols), cols)
            to = pl.ds(pl.multiple_of(t * cols, cols), cols)
            pltpu.make_async_copy(g_hbm.at[:, at], g_v.at[q, :, to], in_sem.at[q]).start()
            return 0

        lax.fori_loop(0, NT, one, 0)

    load_gradient(0)
    states = [
        pltpu.make_async_copy(a, b, st_sem.at[i])
        for i, (a, b) in enumerate(((master_hbm, master_v), (moment_hbm, moment_v), (second_hbm, second_v)))
    ]

    def greetings(stage, devices):
        for device in devices:
            pl.semaphore_signal(greet.at[stage], 1, device_id=device, device_id_type=MESH)

    def remote(src, dst, send, recv, there):
        return pltpu.make_async_remote_copy(src, dst, send, recv, **there)

    def start(*copies):
        for copy in copies:
            copy.start()

    def z1(q):
        return remote(z_own.at[q, 1 - me_z], z_got.at[q], z1_send.at[q], z1_recv.at[q], to_dp(z_mate))

    def zr(q, side):
        part = (Z1, Z2)[side]
        return remote(z_part.at[q, OPPOSITE - 1, part], z_relay.at[q, side], zr_send.at[q], zr_recv.at[q, side],
                      to_y((NEXT, PREVIOUS)[side]))

    def zo(q, side):
        part, k = (Z2, Z1)[side], (NEXT, PREVIOUS)[side]
        return remote(z_part.at[q, k - 1, part], z_last.at[q, side, part], zo_send.at[q], zf_recv.at[q], to_y(k))

    def zs(q, side):
        part, k = (Z1, Z2)[side], (NEXT, PREVIOUS)[side]
        return remote(z_sum.at[q, side], z_last.at[q, side, part], zs_send.at[q], zf_recv.at[q], to_y(k))

    def yr(q, side):
        part = (Y1, Y2)[side]
        return remote(y_own.at[q, y_peer(OPPOSITE), part], y_relay.at[q, side], yr_send.at[q], yr_recv.at[q, side],
                      to_y((NEXT, PREVIOUS)[side]))

    def yo(q, side):
        part, k = (Y2, Y1)[side], (NEXT, PREVIOUS)[side]
        return remote(y_own.at[q, y_peer(k), part], y_got.at[q, side, part], yo_send.at[q], yf_recv.at[q], to_y(k))

    def ys(q, side):
        part, k = (Y1, Y2)[side], (NEXT, PREVIOUS)[side]
        return remote(y_sum.at[q, side], y_got.at[q, side, part], ys_send.at[q], yf_recv.at[q], to_y(k))

    def y2(q):
        return remote(y_part.at[q], y_last.at[q], y2_send.at[q], y2_recv.at[q], to_dp(z_mate))

    def split(q):
        wait_bytes(g_v.at[q], in_sem.at[q])

        def one(t, put):
            for r in range(PR // 16):
                at = pl.multiple_of(t * cols + r * 2048, 2048)
                for u in range(16):
                    spread[u * 8 : u * 8 + 8, :] = g_v[q, :, pl.ds(at + u * TB, TB)].astype(f32)
                for i in range(N_DP):
                    put(i, slice(r * 16, r * 16 + 16), spread[pl.ds(i, 16, stride=8), :].astype(bf16))

        def one_z(a, _):
            def put(i, rows, value):
                z_own[q, i % 2, i // 2, a, rows, :] = value

            one(a, put)
            return 0

        def one_y(b, _):
            def put(i, rows, value):
                y_own[q, i // 2, b, i % 2, rows, :] = value

            one(b + NZ, put)
            return 0

        lax.fori_loop(0, NY, one_y, 0)
        lax.fori_loop(0, NZ, one_z, 0)
        if q == 0:
            pl.semaphore_wait(barrier, len(near))
        start(yr(q, 0), yr(q, 1), yo(q, 0), yo(q, 1), z1(q))
        if q == 0:
            greetings(0, x_next)
            for p in range(1, PIECES):
                load_gradient(p)
            start(*states)

    def wide(x):
        return x.astype(f32)

    def y_relay_step(q):
        yr(q, 0).wait_recv()
        yr(q, 1).wait_recv()

        def add(b, _):
            y_sum[q, 0, b] = (wide(y_own[q, y_peer(NEXT), b]) + wide(y_relay[q, 0, b])).astype(bf16)
            y_sum[q, 1, b] = (wide(y_own[q, y_peer(PREVIOUS), b + YH]) + wide(y_relay[q, 1, b])).astype(bf16)
            return 0

        lax.fori_loop(0, YH, add, 0, unroll=2)
        start(ys(q, 0), ys(q, 1))

    def z_middle(q):
        z1(q).wait_recv()
        for k in (OPPOSITE, NEXT, PREVIOUS):
            y = y_peer(k)
            z_part[q, k - 1] = (wide(z_own[q, me_z, y]) + wide(z_got[q, y])).astype(bf16)
        start(zr(q, 0), zr(q, 1), zo(q, 0), zo(q, 1))

    def z_relay_step(q):
        zr(q, 0).wait_recv()
        zr(q, 1).wait_recv()
        z_sum[q, 0] = (wide(z_part[q, NEXT - 1, Z1]) + wide(z_relay[q, 0])).astype(bf16)
        z_sum[q, 1] = (wide(z_part[q, PREVIOUS - 1, Z2]) + wide(z_relay[q, 1])).astype(bf16)
        start(zs(q, 0), zs(q, 1))

    def y_middle(q):
        wait_bytes(y_got.at[q], yf_recv.at[q])
        for part in (Y1, Y2):
            total = wide(y_own[q, me_y, part, 1 - me_z])
            for side in range(2):
                total = total + wide(y_got[q, side, part, 1 - me_z])
            y_part[q, part] = total.astype(bf16)
        y2(q).start()

    def update(q):
        wait_bytes(z_last.at[q], zf_recv.at[q])
        y2(q).wait_recv()
        if q == 0:
            for copy in states:
                copy.wait()
        rows = slice(q * PR, q * PR + PR)
        groups = [(0, NZ, None)] + [(NZ + part.start, NZ + part.stop, part) for part in (Y1, Y2)]
        for first, stop, part in groups:
            if part is None:
                terms = [z_own[q, me_z, me_y], z_got[q, me_y], z_last[q, 0], z_last[q, 1]]
            else:
                terms = [y_own[q, me_y, part, me_z], y_got[q, 0, part, me_z], y_got[q, 1, part, me_z], y_last[q, part]]
            grad = functools.reduce(lambda a, b: a + b, [wide(x) for x in terms])
            tiles = slice(first, stop)
            new = adam(grad, master_v[tiles, rows, :], moment_v[tiles, rows, :], second_v[tiles, rows, :])
            master_out[tiles, rows, :], moment_out[tiles, rows, :], second_out[tiles, rows, :] = new
            narrow[q][tiles] = new[0].astype(bf16)
            size = jnp.abs(new[0])
            largest[tiles] = size if q == 0 else jnp.maximum(largest[tiles], size)
        if q == PIECES - 1:
            for t in range(NT):
                peak = jnp.max(jnp.max(largest[t], axis=0, keepdims=True), axis=1, keepdims=True)
                rounded = (jnp.broadcast_to(peak, (16, TB)) + scale_epsilon).astype(bf16)
                scale[t] = wide(rounded)[0:1, :]

    def shard_copy(p, k):
        return remote(stage.at[p, k - 1], arrive[p].at[k - 1], sh_send.at[p], sh_recv.at[p],
                      dict(device_id={"shard": sh_peer(k)}, device_id_type=MESH))

    def scale_copy(k):
        return remote(stage_s.at[k - 1], arrive_s.at[k - 1], ss_send, ss_recv,
                      dict(device_id={"shard": sh_peer(k)}, device_id_type=MESH))

    def to_owners(p):
        def stage_step(k, _):
            stage[p, k - 1] = narrow[p][idx_s[k - 1, 0]]
            if p == PIECES - 1:
                stage_s[k - 1] = scale[idx_s[k - 1, 0]]
                scale_copy(k).start()
            shard_copy(p, k).start()
            return 0

        lax.fori_loop(1, N_SH, stage_step, 0)
        arrive[p][N_SH - 1] = narrow[p][idx_s[N_SH - 1, 0]]
        if p == PIECES - 1:
            arrive_s[N_SH - 1] = scale[idx_s[N_SH - 1, 0]]

    def block_copy(p, d, n, there):
        return remote(whole.at[p, d], whole.at[p, d], ag_send.at[p, n], ag_recv.at[p, n], there)

    def gather_copy(p, n):
        k = (None, NEXT, PREVIOUS, NEXT, PREVIOUS, NEXT, PREVIOUS)[n]
        if n == 0:
            return block_copy(p, me_dp, n, to_dp(z_mate))
        block = me_dp if n < 3 else z_mate
        if n == 5:
            block = y_peer(PREVIOUS) * 2 + me_z
        if n == 6:
            block = y_peer(NEXT) * 2 + 1 - me_z
        return block_copy(p, block, n, to_y(k))

    def gather_scale_copy(k):
        return remote(whole_s.at[me_dp], whole_s.at[me_dp], as_send.at[k], as_recv.at[k], to_dp(dp_peer(k)))

    def pack(p):
        if p == PIECES - 1:
            wait_bytes(arrive_s.at[pl.ds(0, N_SH - 1)], ss_recv)
            for i in range(NT):
                whole_s[me_dp, i] = arrive_s[idx_s[N_SH + i, 0]]
            for k in range(1, N_DP):
                gather_scale_copy(k).start()
        wait_bytes(arrive[p].at[pl.ds(0, N_SH - 1)], sh_recv.at[p])
        for i in range(NT):
            whole[p, me_dp, i] = arrive[p][idx_s[N_SH + i, 0]]
        start(gather_copy(p, 0), gather_copy(p, 1), gather_copy(p, 2))

    def pass_mate(p):
        gather_copy(p, 0).wait_recv()
        start(gather_copy(p, 3), gather_copy(p, 4))

    def pass_same(p):
        gather_copy(p, 1).wait_recv()
        gather_copy(p, 5).start()

    def pass_other(p):
        gather_copy(p, 4).wait_recv()
        gather_copy(p, 6).start()

    def tables(_):
        index_tables(tab_ref, idx_v, place, me_sh, me_dp)
        copy = pltpu.make_async_copy(idx_v, idx_s, idx_sem)
        copy.start()
        copy.wait()

    def meet(n):
        pl.semaphore_wait(greet.at[n], 2 if n < 3 else 1)
        if n < 3:
            greetings(n + 1, h_next if n < 2 else [core_mate])

    acts = {
        "S": split, "r": y_relay_step, "m": z_middle, "s": z_relay_step, "n": y_middle, "L": update,
        "T": to_owners, "P": pack, "M": pass_mate, "N": pass_same, "O": pass_other, "x": tables, "g": meet,
    }
    for step in STEPS:
        acts[step[0]](int(step[1:]))

    for q in range(PIECES):
        z1(q).wait_send()
        y2(q).wait_send()
        for side in range(2):
            for copy in (zr, zo, zs, yr, yo, ys):
                copy(q, side).wait_send()
        wait_bytes(stage.at[q, pl.ds(0, N_SH - 1)], sh_send.at[q])
        for n in range(7):
            gather_copy(q, n).wait_send()
        for n in (2, 3, 5, 6):
            gather_copy(q, n).wait_recv()
    wait_bytes(stage_s.at[pl.ds(0, N_SH - 1)], ss_send)
    for k in range(1, N_DP):
        gather_scale_copy(k).wait()


def place_kernel(
    whole, whole_s, place, master_v, moment_v, second_v, tiles, scales, master_out, moment_out, second_out,
    ready, sem, tile_sem,
):
    copies = [
        pltpu.make_async_copy(a, b, sem.at[i])
        for i, (a, b) in enumerate(((master_v, master_out), (moment_v, moment_out), (second_v, second_out)))
    ]
    lane = lax.broadcasted_iota(jnp.int32, (1, TB), 1)

    def step(s, row):
        at = place[s, 0]
        tile_scale = whole_s[at]
        inverse = jnp.broadcast_to(1.0 / tile_scale, (PR, TB))
        ready[s] = (whole[:, at].astype(jnp.float32) * inverse).astype(jnp.bfloat16)
        pltpu.make_async_copy(ready.at[s], tiles.at[s], tile_sem).start()
        return jnp.where(lane == s, tile_scale, row)

    row = lax.fori_loop(0, OWNED, step, jnp.zeros((1, TB), jnp.float32), unroll=8)
    for copy in copies:
        copy.start()
    scales[...] = row.astype(jnp.bfloat16)[0, :OWNED]
    wait_bytes(tiles, tile_sem)
    for copy in copies:
        copy.wait()


def per_device(gradients, tile_table, master, moment, second):
    shape = master.shape
    flat = (NT, TB, TB)
    f32, bf16 = jnp.float32, jnp.bfloat16
    anywhere = pl.BlockSpec(memory_space=pltpu.HBM)
    vmem = pl.BlockSpec(memory_space=pltpu.VMEM)
    smem = pl.BlockSpec(memory_space=pltpu.SMEM)
    dma = pltpu.SemaphoreType.DMA
    state = jax.ShapeDtypeStruct(flat, f32)
    piece = (PR, TB)
    outs = pl.pallas_call(
        main_kernel,
        out_shape=(
            pltpu.VMEM(flat, f32), pltpu.VMEM(flat, f32), pltpu.VMEM(flat, f32),
            pltpu.VMEM((PIECES, N_DP, NT, PR, TB), bf16),
            pltpu.VMEM((N_DP, NT, 1, TB), f32),
            pltpu.VMEM((OWNED, TB), jnp.int32),
        ),
        in_specs=[anywhere, vmem, anywhere, anywhere, anywhere],
        out_specs=(vmem,) * 6,
        scratch_shapes=[
            pltpu.VMEM((PIECES, N_DP, NT * PR * TB), bf16),
            pltpu.VMEM((TB, TB), f32),
            pltpu.VMEM((PIECES, 2, 4, NZ) + piece, bf16),
            pltpu.VMEM((PIECES, 4, NZ) + piece, bf16),
            pltpu.VMEM((PIECES, 3, NZ) + piece, bf16),
            pltpu.VMEM((PIECES, 2, NZ // 2) + piece, bf16),
            pltpu.VMEM((PIECES, 2, NZ // 2) + piece, bf16),
            pltpu.VMEM((PIECES, 2, NZ) + piece, bf16),
            pltpu.VMEM((PIECES, 4, NY, 2) + piece, bf16),
            pltpu.VMEM((PIECES, 2, NY // 2, 2) + piece, bf16),
            pltpu.VMEM((PIECES, 2, NY // 2, 2) + piece, bf16),
            pltpu.VMEM((PIECES, 2, NY, 2) + piece, bf16),
            pltpu.VMEM((PIECES, NY) + piece, bf16),
            pltpu.VMEM((PIECES, NY) + piece, bf16),
            pltpu.VMEM(flat, f32), pltpu.VMEM(flat, f32), pltpu.VMEM(flat, f32),
            pltpu.VMEM((NT,) + piece, f32),
            pltpu.VMEM((NT, 1, TB), f32),
            pltpu.VMEM((PIECES, N_SH) + piece, bf16),
            pltpu.VMEM((N_SH, 1, TB), f32),
            pltpu.VMEM((N_SH, 1, TB), f32),
            pltpu.VMEM((48, TB), jnp.int32),
            pltpu.SMEM((48, TB), jnp.int32),
            *[pltpu.VMEM((N_SH,) + piece, bf16)] * PIECES,
            *[pltpu.VMEM((NT,) + piece, bf16)] * PIECES,
            dma((PIECES,)), dma((3,)), dma(()),
            *[dma((PIECES,))] * 3, dma((PIECES, 2)), *[dma((PIECES,))] * 3,
            dma((PIECES,)), dma((PIECES, 2)), *[dma((PIECES,))] * 5,
            dma((PIECES,)), dma((PIECES,)),
            dma(()), dma(()),
            dma((PIECES, 7)), dma((PIECES, 7)),
            dma((N_DP,)), dma((N_DP,)),
            pltpu.SemaphoreType.REGULAR((4,)),
        ],
        compiler_params=pltpu.CompilerParams(collective_id=0, has_side_effects=True, vmem_limit_bytes=58 << 20),
    )(
        gradients.reshape(N_DP, NT * TB * TB), tile_table,
        master.reshape(flat), moment.reshape(flat), second.reshape(flat),
    )
    master_new, moment_new, second_new, whole, whole_s, place = outs
    tiles, scales, master_new, moment_new, second_new = pl.pallas_call(
        place_kernel,
        out_shape=(
            jax.ShapeDtypeStruct((OWNED, PIECES, PR, TB), bf16),
            jax.ShapeDtypeStruct((OWNED,), bf16),
            state, state, state,
        ),
        in_specs=[vmem, vmem, smem, vmem, vmem, vmem],
        out_specs=(anywhere, vmem, anywhere, anywhere, anywhere),
        scratch_shapes=[pltpu.VMEM((OWNED, PIECES) + piece, bf16), dma((3,)), dma(())],
        compiler_params=pltpu.CompilerParams(vmem_limit_bytes=16 << 20),
    )(whole.reshape(PIECES, OWNED, PR, TB), whole_s.reshape(OWNED, 1, TB), place, master_new, moment_new, second_new)
    return (
        master_new.reshape(shape), moment_new.reshape(shape), second_new.reshape(shape),
        tiles.reshape(OWNED, TB, TB), scales,
    )


def solution(mesh):
    in_specs = (
        P("dp", "shard", None, None),
        P(),
        P("shard", "dp", None),
        P("shard", "dp", None),
        P("shard", "dp", None),
    )
    out_specs = (
        P("shard", "dp", None),
        P("shard", "dp", None),
        P("shard", "dp", None),
        P("shard", None, None),
        P("shard"),
    )
    return jax.shard_map(
        per_device, mesh=mesh, in_specs=in_specs, out_specs=out_specs, check_vma=False
    )
```
